512 devices in a mesh: region: 4 (over z_lo), group: 16 (over z_hi, y), loop: 8 (over x, core).
Axes of the slice: x: 4, y: 8, z: 8 (z_hi: 2, z_lo: 4; z = z_hi * 4 + z_lo), core: 2. Of those that a mesh axis runs over, the one named last changes fastest.
Arguments:
- history: float32 [16, 262144], P(None, ('region', 'group', 'loop')), may hold values from -6 to 6
- incident: float32 [4, 262144], P(None, ('region', 'group', 'loop')), may hold values from -6 to 6
- positions: float32 [3, 262144], P(None, ('region', 'group', 'loop')), may hold values from -1 to 1
- area: float32 [262144], P(('region', 'group', 'loop')), may hold values from 0.00390625 to 0.03125
- self_weight: float32 [262144], P(('region', 'group', 'loop')), may hold values from 1 to 2
- pair_target: int32 [512, 24], P(('region', 'group', 'loop')), may hold values from 0 to 31
- pair_source: int32 [512, 24], P(('region', 'group', 'loop')), may hold values from 0 to 7
- pair_lag: int32 [512, 24], P(('region', 'group', 'loop')), may hold values from 1 to 12
- pair_count: int32 [512], P(('region', 'group', 'loop')), may hold values from 16 to 24, as said below
- junc_send: int32 [512, 128], P(('region', 'group', 'loop')), may hold values from 0 to 511
- junc_recv: int32 [512, 128], P(('region', 'group', 'loop')), may hold values from 0 to 511
- junc_gain: float32 [512, 128], P(('region', 'group', 'loop')), may hold values from 0.5 to 2
- adjacency: int32 [512], P(('region', 'group', 'loop')), may hold values from 1 to 3
Outputs:
- density: float32 [4, 262144], P(None, ('region', 'group', 'loop'))
The draws below stay inside these ranges and needn't reach their ends.
Inputs may be any that keep to these rules, and one draw needn't show every extreme that they name: `pair_count`: each device uses between 16 and 24 of its listed pairs, and some device uses all 24.
All inputs are finite; a program needn't handle non-finite values.
Results may differ from the reference program's by a relative error of at most 0.0003.
Values sent between devices are 32-bit elements; how exact they have to be, the bound alone decides.
No kernel may reach another device: no remote copies, remote signals or barrier semaphores. Data moves between devices by JAX's collectives and lax.ppermute only.
A program may use at most 64 MiB of HBM per device.

```python
import math
import jax
import jax.numpy as jnp
from jax import lax

NODE_DEV = 512
HIST = 16
STEPS = 4
PAIRS = 24
JROWS = 128
TILE_ROWS = 256
REGIONS = 4
GROUPS = 16
LOOPS = 8
DEVICE_COUNT = 512
NODES = 262144


def draw_pair_count(key, part):
    base = jax.random.randint(key, (DEVICE_COUNT,), 16, PAIRS + 1)
    heavy = jax.random.randint(jax.random.fold_in(key, 1), (DEVICE_COUNT,), 0, 8) == 0
    chosen = jax.random.randint(jax.random.fold_in(key, 2), (), 0, DEVICE_COUNT)
    heavy = heavy | (jnp.arange(DEVICE_COUNT) == chosen)
    return jnp.where(heavy, PAIRS, base).astype(jnp.int32)


def touch_ends(entries, stream_key, low, largest):
    index_at = [jax.random.randint(jax.random.fold_in(stream_key, axis), (), 0, length) for axis, length in enumerate(entries.shape)]
    longest = entries.shape.index(max(entries.shape))
    next_to = index_at[:longest] + [(index_at[longest] + 1) % entries.shape[longest]] + index_at[longest + 1:]
    return entries.at[tuple(index_at)].set(low).at[tuple(next_to)].set(largest)


def block_levels(stream_key, extent, pieces, low, high):
    loudness, own = 1.0, jax.random.fold_in(stream_key, 6)
    for axis_at, blocks in pieces:
        heights = jnp.exp(jax.random.uniform(jax.random.fold_in(own, axis_at), (blocks,), jnp.float32, low / len(pieces), high / len(pieces)))
        loudness = loudness * jnp.repeat(heights, extent[axis_at] // blocks).reshape([-1 if axis == axis_at else 1 for axis in range(len(extent))])
    return loudness


def normal_values(key, shape, spread, most, cuts=(), kind=jnp.bfloat16):
    values = jax.random.normal(key, shape, jnp.float32) * spread
    if len(cuts) > 0:
        values = block_levels(key, shape, cuts, -0.22, 0.18) * values
    return jnp.clip(values, min=-most, max=most).astype(kind)


def setup_inputs(seed: int = 0) -> dict:
    key_list = jax.random.split(jax.random.key(seed), 14)
    history = normal_values(key_list[0], (HIST, NODES), 1.0, 6.0, ((1, 512),), jnp.float32)
    incident = normal_values(key_list[1], (STEPS, NODES), 1.0, 6.0, ((1, 512),), jnp.float32)
    positions = jnp.clip(jax.random.uniform(key_list[2], (3, NODES), jnp.float32, -1.0, 1.0) * block_levels(key_list[2], (3, NODES), ((1, 512),), -0.4, 0.0), -1.0, 1.0)
    area = jnp.clip(jnp.exp(math.log(0.03125) - 2.0794415 * jax.random.uniform(key_list[3], (NODES,), jnp.float32) ** block_levels(key_list[3], (NODES,), ((0, 512),), -0.2, 0.2)), 0.00390625, 0.03125)
    self_weight = jnp.clip(1.0 + 1.0 * jax.random.uniform(key_list[4], (NODES,), jnp.float32) ** block_levels(key_list[4], (NODES,), ((0, 512),), -0.2, 0.2), 1.0, 2.0)
    pair_target = touch_ends(jax.random.randint(key_list[5], (DEVICE_COUNT, PAIRS), 0, 2 * GROUPS), jax.random.fold_in(key_list[5], 1), 0, (2 * GROUPS) - 1).astype(jnp.int32)
    pair_source = touch_ends(jax.random.randint(key_list[6], (DEVICE_COUNT, PAIRS), 0, LOOPS), jax.random.fold_in(key_list[6], 1), 0, LOOPS - 1).astype(jnp.int32)
    pair_lag = touch_ends(jax.random.randint(key_list[7], (DEVICE_COUNT, PAIRS), 1, HIST - 3), jax.random.fold_in(key_list[7], 1), 1, (HIST - 3) - 1).astype(jnp.int32)
    pair_count = draw_pair_count(jax.random.fold_in(key_list[13], 71), 0)
    junc_send = touch_ends(jax.random.randint(key_list[9], (DEVICE_COUNT, JROWS), 0, NODE_DEV), jax.random.fold_in(key_list[9], 1), 0, NODE_DEV - 1).astype(jnp.int32)
    junc_recv = touch_ends(jax.random.randint(key_list[10], (DEVICE_COUNT, JROWS), 0, NODE_DEV), jax.random.fold_in(key_list[10], 1), 0, NODE_DEV - 1).astype(jnp.int32)
    junc_gain = jnp.clip(jnp.exp(math.log(2.0) - 1.3862944 * jax.random.uniform(key_list[11], (DEVICE_COUNT, JROWS), jnp.float32) ** block_levels(key_list[11], (DEVICE_COUNT, JROWS), ((0, 512),), -0.2, 0.2)), 0.5, 2.0)
    adjacency = touch_ends(jax.random.randint(key_list[12], (DEVICE_COUNT,), 1, REGIONS), jax.random.fold_in(key_list[12], 1), 1, REGIONS - 1).astype(jnp.int32)
    return {"history": history, "incident": incident, "positions": positions, "area": area, "self_weight": self_weight, "pair_target": pair_target, "pair_source": pair_source, "pair_lag": pair_lag, "pair_count": pair_count, "junc_send": junc_send, "junc_recv": junc_recv, "junc_gain": junc_gain, "adjacency": adjacency}


soften = 0.25

def spline_mix(frac, rows):
    one_minus = 1.0 - frac
    cube = frac * frac * frac
    square = frac * frac
    first = one_minus * one_minus * one_minus / 6.0
    second = (3.0 * cube - 6.0 * square + 4.0) / 6.0
    third = (-3.0 * cube + 3.0 * square + 3.0 * frac + 1.0) / 6.0
    fourth = cube / 6.0
    return first * rows[3][None, :] + second * rows[2][None, :] + third * rows[1][None, :] + fourth * rows[0][None, :]

def pair_term(target_pos, source_pos, source_area, rows):
    delta = target_pos[:, :, None] - source_pos[:, None, :]
    dist_sq = lax.optimization_barrier(jnp.sum(delta * delta, axis=0))
    weight = source_area[None, :] * lax.rsqrt(dist_sq + soften)
    frac = dist_sq / (1.0 + dist_sq)
    return lax.optimization_barrier(jnp.sum(weight * spline_mix(frac, rows), axis=1))

def reference(history, incident, positions, area, self_weight, pair_target, pair_source, pair_lag, pair_count, junc_send, junc_recv, junc_gain, adjacency):
    stored = jnp.concatenate([history, jnp.zeros((STEPS, NODES), jnp.float32)], axis=0)
    block_ids = jnp.arange(DEVICE_COUNT, dtype=jnp.int32)
    per_region = GROUPS * LOOPS
    for step in range(STEPS):

        def device_step(field, block):
            region_id = block // per_region
            group_id = block // LOOPS % GROUPS
            loop_id = block % LOOPS

            def pair_fn(index, acc):
                tile = pair_target[block, index]
                member = pair_source[block, index]
                lag = pair_lag[block, index]
                first_row = tile * TILE_ROWS
                target_group = first_row // NODE_DEV
                offset = first_row % NODE_DEV
                target_row = (((region_id * GROUPS + target_group) * LOOPS + loop_id) * NODE_DEV + offset).astype(jnp.int32)
                source_row = (((region_id * GROUPS + group_id) * LOOPS + member) * NODE_DEV).astype(jnp.int32)
                zero = jnp.zeros((), jnp.int32)
                target_pos = lax.dynamic_slice(positions, (zero, target_row), (3, TILE_ROWS))
                source_pos = lax.dynamic_slice(positions, (zero, source_row), (3, NODE_DEV))
                source_area = lax.dynamic_slice(area, (source_row,), (NODE_DEV,))
                start = (HIST + step - lag - 3).astype(jnp.int32)
                rows = lax.dynamic_slice(stored, (start, source_row), (4, NODE_DEV))
                term = pair_term(target_pos, source_pos, source_area, rows)
                current = lax.dynamic_slice(acc, (target_row,), (TILE_ROWS,))
                return lax.dynamic_update_slice(acc, current + term, (target_row,))
            return (lax.fori_loop(0, pair_count[block], pair_fn, field), None)
        field, _ = lax.scan(device_step, jnp.zeros((NODES,), jnp.float32), block_ids)
        previous = stored[HIST + step - 1].reshape(DEVICE_COUNT, NODE_DEV)
        traces = jnp.take_along_axis(previous, junc_send, axis=1)
        partner_region = (block_ids // per_region + adjacency) % REGIONS
        partner = (partner_region * per_region + block_ids % per_region).astype(jnp.int32)
        received = traces[partner]
        junction = jnp.zeros((DEVICE_COUNT, NODE_DEV), jnp.float32).at[block_ids[:, None], junc_recv].add(junc_gain * received)
        density_now = (incident[step] - field - junction.reshape(NODES)) / self_weight
        stored = stored.at[HIST + step].set(density_now)
    return stored[HIST:]
```

```python
import functools

import jax
import jax.numpy as jnp
from jax import lax
from jax.experimental import pallas as pl
from jax.experimental.pallas import tpu as pltpu
from jax.sharding import PartitionSpec as P

HIST = 16
STEPS = 4
LANES = 128
SUBS = 8
SOFTEN = 0.25
AREA_ROW = 3
STORED_ROW = 4
SOURCE_ROWS = 24
COEFS = 4


VMEM = pl.BlockSpec(memory_space=pltpu.VMEM)
SMEM = pl.BlockSpec(memory_space=pltpu.SMEM)


def spline_coefs(rows, scale):
    d, c, b, a = rows
    return (
        (b + 4.0 * c + d) * scale,
        3.0 * (b - d) * scale,
        3.0 * (b - 2.0 * c + d) * scale,
        (a - d + 3.0 * (c - b)) * scale,
    )


def fill_targets(tile_ref, tcol_ref):
    tcol_ref[...] = jnp.transpose(tile_ref[...], (1, 0))


def pair_sums(steps, nodes, tcol_ref, geo_ref, coef_ref, res_ref):
    blocks = nodes // LANES
    lane = lax.broadcasted_iota(jnp.int32, (SUBS, LANES), 1)

    def block_fn(i, carry):
        rows = pl.ds(pl.multiple_of(i * SUBS, SUBS), SUBS)
        tcol = tcol_ref[rows, :]
        coords = [jnp.broadcast_to(tcol[:, k : k + 1], (SUBS, LANES)) for k in range(3)]
        sums = [None] * steps
        for c in range(blocks):
            cols = slice(c * LANES, (c + 1) * LANES)
            dist_sq = None
            for k in range(3):
                delta = coords[k] - geo_ref[k, :, cols]
                square = delta * delta
                dist_sq = square if dist_sq is None else dist_sq + square
            weight = lax.rsqrt(dist_sq + SOFTEN)
            u = 1.0 / (1.0 + dist_sq)
            for n in range(steps):
                mix = coef_ref[n * COEFS + 3, :, cols]
                for power in (2, 1, 0):
                    mix = mix * u + coef_ref[n * COEFS + power, :, cols]
                term = weight * mix
                sums[n] = term if sums[n] is None else sums[n] + term
        value = jnp.zeros((SUBS, LANES), jnp.float32)
        for n in range(steps):
            value = jnp.where(lane == n, jnp.sum(sums[n], axis=1, keepdims=True), value)
        res_ref[rows, :] = value
        return carry

    lax.fori_loop(0, res_ref.shape[0] // SUBS, block_fn, 0, unroll=2)


def spread(ref, index, row):
    ref[index, :, :] = jnp.broadcast_to(row, ref.shape[1:])


def history_kernel(count_ref, target_ref, source_ref, lag_ref, tgt_ref, src_ref, out_ref, tcol, geo, coef, res):
    nodes = src_ref.shape[2]
    out_ref[...] = jnp.zeros_like(out_ref)

    def pair_fn(p, carry):
        tile, member, lag = target_ref[0, p], source_ref[0, p], lag_ref[0, p]
        fill_targets(tgt_ref.at[tile], tcol)
        for k in range(3):
            spread(geo, k, src_ref[member, k : k + 1, :])
        scale = src_ref[member, AREA_ROW : AREA_ROW + 1, :] * (1.0 / 6.0)
        first = STORED_ROW + HIST - 3 - lag
        window = [src_ref[member, pl.ds(first + i, 1), :] for i in range(STEPS + 3)]
        for n in range(STEPS):
            for power, value in enumerate(spline_coefs(window[n : n + 4], scale)):
                spread(coef, n * COEFS + power, value)
        pair_sums(STEPS, nodes, tcol, geo, coef, res)
        out_ref[tile] += jnp.transpose(res[...], (1, 0))[:STEPS, :]
        return carry

    lax.fori_loop(0, count_ref[0], pair_fn, 0)


def step_kernel(step, count_ref, target_ref, source_ref, lag_ref, tgt_ref, src_ref, *refs):
    new_refs = refs[:step]
    out_ref, tcol, geo, coef, res, new = refs[step:]
    nodes = src_ref.shape[2]
    out_ref[...] = jnp.zeros_like(out_ref)
    new[...] = jnp.zeros_like(new)
    for j in range(step):
        new[:, 3 + j, :] = new_refs[j][...]

    def pair_fn(p, carry):
        tile, member, lag = target_ref[0, p], source_ref[0, p], lag_ref[0, p]

        @pl.when(lag <= step)
        def _():
            fill_targets(tgt_ref.at[tile], tcol)
            for k in range(3):
                spread(geo, k, src_ref[member, k : k + 1, :])
            scale = src_ref[member, AREA_ROW : AREA_ROW + 1, :] * (1.0 / 6.0)
            window = [new[member, pl.ds(step - lag + i, 1), :] for i in range(4)]
            for power, value in enumerate(spline_coefs(window, scale)):
                spread(coef, power, value)
            pair_sums(1, nodes, tcol, geo, coef, res)
            row = pl.ds(tile, 1)
            out_ref[row, :] += jnp.transpose(res[...], (1, 0))[:1, :]

        return carry

    lax.fori_loop(0, count_ref[0], pair_fn, 0)


def dot_exact(a, b, dims):
    return lax.dot_general(a, b, (dims, ((), ())), precision=lax.Precision.HIGHEST, preferred_element_type=jnp.float32)


def pick_trace(density, send_ref):
    nodes, rows = density.shape[1], send_ref.shape[1]
    node = lax.broadcasted_iota(jnp.int32, (nodes, rows), 0)
    chosen = jnp.where(node == send_ref[...], 1.0, 0.0)
    return dot_exact(jnp.broadcast_to(density, (SUBS, nodes)), chosen, ((1,), (0,)))[:1, :]


def junction_of(partner, trace_ref, recv_ref, gain_ref, nodes):
    rows = recv_ref.shape[1]
    node = lax.broadcasted_iota(jnp.int32, (nodes, rows), 0)
    chosen = jnp.where(node == recv_ref[...], 1.0, 0.0)
    trace = trace_ref[pl.ds(partner, 1), :] * gain_ref[...]
    return dot_exact(jnp.broadcast_to(trace, (SUBS, rows)), chosen, ((1,), (1,)))[:1, :]


def first_trace_kernel(send_ref, hist_ref, trace_ref):
    trace = pick_trace(hist_ref[HIST - 1 : HIST, :], send_ref)
    trace_ref[...] = jnp.broadcast_to(trace, trace_ref.shape)


def density_kernel(step, partner_ref, part_ref, trace_ref, send_ref, recv_ref, gain_ref, inc_ref, self_ref, *refs):
    nodes = inc_ref.shape[1]
    if step == 0:
        dens_ref, next_ref, past_ref = refs
        halves = []
        for h in range(2):
            total = part_ref[h]
            for g in range(1, part_ref.shape[0] // 2):
                total = total + part_ref[2 * g + h]
            halves.append(total)
        past = jnp.concatenate(halves, axis=1)
        past_ref[...] = past
        field = past[:1, :]
    else:
        past_ref, dens_ref = refs[:2]
        next_ref = refs[2] if step < STEPS - 1 else None
        halves = []
        for h in range(2):
            total = part_ref[h : h + 1, :]
            for g in range(1, part_ref.shape[0] // 2):
                total = total + part_ref[2 * g + h : 2 * g + h + 1, :]
            halves.append(total)
        field = past_ref[step : step + 1, :] + jnp.concatenate(halves, axis=1)
    junction = junction_of(partner_ref[0], trace_ref, recv_ref, gain_ref, nodes)
    density = (inc_ref[step : step + 1, :] - field - junction) / self_ref[...]
    dens_ref[...] = jnp.broadcast_to(density, dens_ref.shape)
    if next_ref is not None:
        trace = pick_trace(density, send_ref)
        next_ref[...] = jnp.broadcast_to(trace, next_ref.shape)


def body(
    history,
    incident,
    positions,
    area,
    self_weight,
    pair_target,
    pair_source,
    pair_lag,
    pair_count,
    junc_send,
    junc_recv,
    junc_gain,
    adjacency,
):
    nodes = history.shape[1]
    half = nodes // 2
    jrows = junc_send.shape[1]
    groups, regions, loops = (lax.axis_size(name) for name in ("group", "region", "loop"))
    tiles = 2 * groups
    f32 = jnp.float32
    shape = jax.ShapeDtypeStruct
    partner = ((lax.axis_index("region") + adjacency) % regions).astype(jnp.int32)
    self_row = self_weight.reshape(1, nodes)
    lists = (pair_count, pair_target, pair_source, pair_lag)

    packed = jnp.concatenate(
        [positions, area[None], history, jnp.zeros((SOURCE_ROWS - STORED_ROW - HIST, nodes), f32)], axis=0
    )
    sources = lax.all_to_all(jnp.broadcast_to(packed, (loops, SOURCE_ROWS, nodes)), "loop", 0, 0, tiled=True)
    mine = jnp.pad(positions, ((0, SUBS - 3), (0, 0))).reshape(SUBS, 2, half).transpose(1, 0, 2)
    targets = lax.all_to_all(
        jnp.broadcast_to(mine[None], (groups, 2, SUBS, half)).reshape(tiles, SUBS, half), "group", 0, 0, tiled=True
    )
    trace = pl.pallas_call(
        first_trace_kernel, out_shape=shape((regions, jrows), f32), in_specs=[VMEM] * 2, out_specs=VMEM
    )(junc_send, history)

    work = [
        pltpu.VMEM((half, SUBS), f32),
        pltpu.VMEM((3, SUBS, nodes), f32),
        pltpu.VMEM((STEPS * COEFS, SUBS, nodes), f32),
        pltpu.VMEM((half, LANES), f32),
    ]
    partial_fields = pl.pallas_call(
        history_kernel,
        out_shape=shape((tiles, STEPS, half), f32),
        in_specs=[SMEM] * 4 + [VMEM] * 2,
        out_specs=VMEM,
        scratch_shapes=work,
    )(*lists, targets, sources)

    outputs = []
    gathered = []
    past = None
    for step in range(STEPS):
        if step > 0:
            partial_fields = pl.pallas_call(
                functools.partial(step_kernel, step),
                out_shape=shape((tiles, half), f32),
                in_specs=[SMEM] * 4 + [VMEM] * (2 + step),
                out_specs=VMEM,
                scratch_shapes=work + [pltpu.VMEM((loops, SUBS, nodes), f32)],
            )(*lists, targets, sources, *gathered)
        parts = lax.all_to_all(partial_fields, "group", 0, 0, tiled=True)
        traces = lax.all_to_all(trace, "region", 0, 0, tiled=True)
        last = step == STEPS - 1
        out_shape = [shape((loops, nodes), f32)]
        if not last:
            out_shape.append(shape((regions, jrows), f32))
        if step == 0:
            out_shape.append(shape((STEPS, nodes), f32))
        operands = [partner, parts, traces, junc_send, junc_recv, junc_gain, incident, self_row]
        if step > 0:
            operands.append(past)
        results = pl.pallas_call(
            functools.partial(density_kernel, step),
            out_shape=out_shape,
            in_specs=[SMEM] + [VMEM] * (len(operands) - 1),
            out_specs=[VMEM] * len(out_shape),
        )(*operands)
        density = results[0]
        if step == 0:
            past = results[2]
        outputs.append(density[0])
        if not last:
            trace = results[1]
            gathered.append(lax.all_to_all(density, "loop", 0, 0, tiled=True))
    return jnp.stack(outputs, axis=0)


def solution(mesh):
    blocks = ("region", "group", "loop")
    in_specs = (
        P(None, blocks),
        P(None, blocks),
        P(None, blocks),
        P(blocks),
        P(blocks),
        P(blocks, None),
        P(blocks, None),
        P(blocks, None),
        P(blocks),
        P(blocks, None),
        P(blocks, None),
        P(blocks, None),
        P(blocks),
    )
    return jax.shard_map(body, mesh=mesh, in_specs=in_specs, out_specs=P(None, blocks), check_vma=False)
```

```python
import functools

import jax
import jax.numpy as jnp
from jax import lax
from jax.experimental import pallas as pl
from jax.experimental.pallas import tpu as pltpu
from jax.sharding import PartitionSpec as P

HIST = 16
STEPS = 4
LANES = 128
SUBS = 8
SOFTEN = 0.25
AREA_ROW = 3
STORED_ROW = 4
SOURCE_ROWS = 24
COEFS = 4


VMEM = pl.BlockSpec(memory_space=pltpu.VMEM)
SMEM = pl.BlockSpec(memory_space=pltpu.SMEM)


def spline_coefs(rows, scale):
    d, c, b, a = rows
    return (
        (b + 4.0 * c + d) * scale,
        3.0 * (b - d) * scale,
        3.0 * (b - 2.0 * c + d) * scale,
        (a - d + 3.0 * (c - b)) * scale,
    )


def spread_targets(tgt_ref, tile, tb_ref):
    group, start = tile // 2, (tile % 2) * 2
    for k in range(3):
        for b in range(2):
            row = tgt_ref[group, pl.ds(4 * k + b + start, 1), :]
            tb_ref[k, b * LANES : (b + 1) * LANES, :] = jnp.transpose(jnp.broadcast_to(row, (LANES, LANES)), (1, 0))


def pair_sums(steps, nodes, tb_ref, geo_ref, coef_ref, acc_ref):
    def block_fn(i, carry):
        rows = pl.ds(pl.multiple_of(i * SUBS, SUBS), SUBS)
        coords = [tb_ref[k, rows, :] for k in range(3)]
        sums = [None] * steps
        for c in range(nodes // LANES):
            cols = slice(c * LANES, (c + 1) * LANES)
            dist_sq = None
            for k in range(3):
                delta = coords[k] - geo_ref[k, :, cols]
                square = delta * delta
                dist_sq = square if dist_sq is None else dist_sq + square
            weight = lax.rsqrt(dist_sq + SOFTEN)
            u = 1.0 / (1.0 + dist_sq)
            for n in range(steps):
                mix = coef_ref[n * COEFS + 3, :, cols]
                for power in (2, 1, 0):
                    mix = mix * u + coef_ref[n * COEFS + power, :, cols]
                term = weight * mix
                sums[n] = term if sums[n] is None else sums[n] + term
        for n in range(steps):
            acc_ref[n, rows, :] = sums[n]
        return carry

    lax.fori_loop(0, acc_ref.shape[1] // SUBS, block_fn, 0, unroll=8)


def lane_totals(acc_ref, n):
    return [
        jnp.sum(jnp.transpose(acc_ref[n, b * LANES : (b + 1) * LANES, :], (1, 0)), axis=0, keepdims=True)
        for b in range(2)
    ]


def spread(ref, index, row):
    ref[index, :, :] = jnp.broadcast_to(row, ref.shape[1:])


def history_kernel(count_ref, target_ref, source_ref, lag_ref, tgt_ref, src_ref, out_ref, tb, geo, coef, acc):
    nodes = src_ref.shape[2]
    out_ref[...] = jnp.zeros_like(out_ref)

    def pair_fn(p, carry):
        tile, member, lag = target_ref[0, p], source_ref[0, p], lag_ref[0, p]
        spread_targets(tgt_ref, tile, tb)
        for k in range(3):
            spread(geo, k, src_ref[member, k : k + 1, :])
        scale = src_ref[member, AREA_ROW : AREA_ROW + 1, :] * (1.0 / 6.0)
        first = STORED_ROW + HIST - 3 - lag
        window = [src_ref[member, pl.ds(first + i, 1), :] for i in range(STEPS + 3)]
        for n in range(STEPS):
            for power, value in enumerate(spline_coefs(window[n : n + 4], scale)):
                spread(coef, n * COEFS + power, value)
        pair_sums(STEPS, nodes, tb, geo, coef, acc)
        totals = [row for n in range(STEPS) for row in lane_totals(acc, n)]
        out_ref[tile] += jnp.concatenate(totals, axis=0)
        return carry

    lax.fori_loop(0, count_ref[0], pair_fn, 0)


def thirds(row):
    high = row.astype(jnp.bfloat16)
    rest = row - high.astype(jnp.float32)
    middle = rest.astype(jnp.bfloat16)
    low = (rest - middle.astype(jnp.float32)).astype(jnp.bfloat16)
    return jnp.concatenate([high, middle, low, jnp.zeros((13, row.shape[1]), jnp.bfloat16)], axis=0)


def one_hot_dot(row, chosen, contract):
    parts = lax.dot_general(thirds(row), chosen, (((1,), (contract,)), ((), ())), preferred_element_type=jnp.float32)
    return parts[0:1, :] + (parts[1:2, :] + parts[2:3, :])


def one_hot(index_ref, nodes):
    node = lax.broadcasted_iota(jnp.int32, (nodes, index_ref.shape[1]), 0)
    return jnp.where(node == index_ref[...], 1.0, 0.0).astype(jnp.bfloat16)


def pick_trace(density, send_ref):
    return one_hot_dot(density, one_hot(send_ref, density.shape[1]), 0)


def junction_of(trace, recv_ref, gain_ref, nodes):
    return one_hot_dot(trace * gain_ref[...], one_hot(recv_ref, nodes), 1)


def step_kernel(
    step, count_ref, target_ref, source_ref, lag_ref, place_ref, tgt_ref, src_ref, send_ref, own_ref, *refs
):
    new_refs = refs[:step]
    out_ref, tb, geo, coef, acc, new = refs[step:]
    nodes = src_ref.shape[2]
    region, group = place_ref[0], place_ref[2]
    out_ref[...] = jnp.zeros_like(out_ref)
    new[...] = jnp.zeros_like(new)
    for j in range(step):
        for r in range(nodes // LANES):
            new[:, 3 + j, r * LANES : (r + 1) * LANES] = new_refs[j][:, r, :]
    trace = pick_trace(own_ref[...], send_ref)
    tiles = tgt_ref.shape[0] * 2
    for other in range(out_ref.shape[0] // tiles):

        @pl.when(other != region)
        def _():
            out_ref[other * tiles + 2 * group] = jnp.concatenate([trace, trace], axis=0)

    def pair_fn(p, carry):
        tile, member, lag = target_ref[0, p], source_ref[0, p], lag_ref[0, p]

        @pl.when(lag <= step)
        def _():
            spread_targets(tgt_ref, tile, tb)
            for k in range(3):
                spread(geo, k, src_ref[member, k : k + 1, :])
            scale = src_ref[member, AREA_ROW : AREA_ROW + 1, :] * (1.0 / 6.0)
            window = [new[member, pl.ds(step - lag + i, 1), :] for i in range(4)]
            for power, value in enumerate(spline_coefs(window, scale)):
                spread(coef, power, value)
            pair_sums(1, nodes, tb, geo, coef, acc)
            out_ref[region * tiles + tile] += jnp.concatenate(lane_totals(acc, 0), axis=0)

        return carry

    lax.fori_loop(0, count_ref[0], pair_fn, 0)


def first_trace_kernel(send_ref, hist_ref, trace_ref):
    trace = pick_trace(hist_ref[HIST - 1 : HIST, :], send_ref)
    for r in range(trace_ref.shape[0]):
        trace_ref[r] = trace


def density_kernel(step, place_ref, part_ref, recv_ref, gain_ref, inc_ref, self_ref, *refs):
    nodes = inc_ref.shape[1]
    region, partner, group = place_ref[0], place_ref[1], place_ref[2]
    last = step == STEPS - 1
    if step == 0:
        trace_ref, dens_ref, row_ref, past_ref = refs
        groups = part_ref.shape[0] // 2
        fields = []
        for h in range(2):
            total = part_ref[h]
            for g in range(1, groups):
                total = total + part_ref[2 * g + h]
            fields.append(total)
        past = jnp.concatenate(fields, axis=0)
        past_ref[...] = past
        trace = trace_ref[partner]
        rows = [past[8 * h + b : 8 * h + b + 1, :] for h in range(2) for b in range(2)]
    else:
        past_ref = refs[0]
        groups = part_ref.shape[0] // 8
        first = region * (2 * groups)
        rows = []
        for h in range(2):
            total = past_ref[8 * h + 2 * step : 8 * h + 2 * step + 2, :]
            for g in range(groups):
                total = total + part_ref[first + 2 * g + h]
            rows += [total[0:1, :], total[1:2, :]]
        trace = part_ref[(partner * groups + group) * 2][0:1, :]
    field = jnp.concatenate(rows, axis=1)
    junction = junction_of(trace, recv_ref, gain_ref, nodes)
    density = (inc_ref[step : step + 1, :] - field - junction) / self_ref[...]
    if last:
        row_refs, out_ref = refs[1:-1], refs[-1]
        for n in range(STEPS - 1):
            out_ref[n : n + 1, :] = row_refs[n][...]
        out_ref[STEPS - 1 : STEPS, :] = density
    else:
        if step > 0:
            dens_ref, row_ref = refs[1:]
        row_ref[...] = density
        for r in range(nodes // LANES):
            part = density[:, r * LANES : (r + 1) * LANES]
            dens_ref[:, r, :] = jnp.broadcast_to(part, (dens_ref.shape[0], LANES))


def body(
    history,
    incident,
    positions,
    area,
    self_weight,
    pair_target,
    pair_source,
    pair_lag,
    pair_count,
    junc_send,
    junc_recv,
    junc_gain,
    adjacency,
):
    nodes = history.shape[1]
    half = nodes // 2
    jrows = junc_send.shape[1]
    groups, regions, loops = (lax.axis_size(name) for name in ("group", "region", "loop"))
    tiles = 2 * groups
    f32 = jnp.float32
    shape = jax.ShapeDtypeStruct
    region = lax.axis_index("region")
    place = jnp.stack([region, (region + adjacency[0]) % regions, lax.axis_index("group")]).astype(jnp.int32)
    self_row = self_weight.reshape(1, nodes)
    lists = (pair_count, pair_target, pair_source, pair_lag)
    line_rows = nodes // LANES

    packed = jnp.concatenate(
        [positions, area[None], history, jnp.zeros((SOURCE_ROWS - STORED_ROW - HIST, nodes), f32)], axis=0
    )
    sources = lax.all_to_all(jnp.broadcast_to(packed, (loops, SOURCE_ROWS, nodes)), "loop", 0, 0, tiled=True)
    mine = positions.reshape(3 * line_rows, LANES)
    targets = lax.all_to_all(jnp.broadcast_to(mine, (groups,) + mine.shape), "group", 0, 0, tiled=True)
    trace = pl.pallas_call(
        first_trace_kernel, out_shape=shape((regions, 1, jrows), f32), in_specs=[VMEM] * 2, out_specs=VMEM
    )(junc_send, history)
    traces = lax.all_to_all(trace, "region", 0, 0, tiled=True)

    def work(steps):
        return [
            pltpu.VMEM((3, half, LANES), f32),
            pltpu.VMEM((3, SUBS, nodes), f32),
            pltpu.VMEM((steps * COEFS, SUBS, nodes), f32),
            pltpu.VMEM((steps, half, LANES), f32),
        ]

    partial_fields = pl.pallas_call(
        history_kernel,
        out_shape=shape((tiles, 2 * STEPS, LANES), f32),
        in_specs=[SMEM] * 4 + [VMEM] * 2,
        out_specs=VMEM,
        scratch_shapes=work(STEPS),
    )(*lists, targets, sources)
    parts = lax.all_to_all(partial_fields, "group", 0, 0, tiled=True)

    dens_shape, row_shape = shape((loops, line_rows, LANES), f32), shape((1, nodes), f32)
    rows, gathered = [], []
    past = None
    for step in range(STEPS):
        if step > 0:
            partial_fields = pl.pallas_call(
                functools.partial(step_kernel, step),
                out_shape=shape((regions * tiles, 2, LANES), f32),
                in_specs=[SMEM] * 5 + [VMEM] * (4 + step),
                out_specs=VMEM,
                scratch_shapes=work(1) + [pltpu.VMEM((loops, SUBS, nodes), f32)],
            )(*lists, place, targets, sources, junc_send, rows[-1], *gathered)
            parts = lax.all_to_all(partial_fields, ("region", "group"), 0, 0, tiled=True)
        operands = [place, parts, junc_recv, junc_gain, incident, self_row]
        if step == 0:
            operands += [traces]
            out_shape = [dens_shape, row_shape, shape((2 * 2 * STEPS, LANES), f32)]
        elif step < STEPS - 1:
            operands += [past]
            out_shape = [dens_shape, row_shape]
        else:
            operands += [past] + rows
            out_shape = [shape((STEPS, nodes), f32)]
        results = pl.pallas_call(
            functools.partial(density_kernel, step),
            out_shape=out_shape,
            in_specs=[SMEM] + [VMEM] * (len(operands) - 1),
            out_specs=[VMEM] * len(out_shape),
        )(*operands)
        if step == 0:
            past = results[2]
        if step < STEPS - 1:
            rows.append(results[1])
            gathered.append(lax.all_to_all(results[0], "loop", 0, 0, tiled=True))
    return results[0]


def solution(mesh):
    blocks = ("region", "group", "loop")
    in_specs = (
        P(None, blocks),
        P(None, blocks),
        P(None, blocks),
        P(blocks),
        P(blocks),
        P(blocks, None),
        P(blocks, None),
        P(blocks, None),
        P(blocks),
        P(blocks, None),
        P(blocks, None),
        P(blocks, None),
        P(blocks),
    )
    return jax.shard_map(body, mesh=mesh, in_specs=in_specs, out_specs=P(None, blocks), check_vma=False)
```

```python
import functools

import jax
import jax.numpy as jnp
from jax import lax
from jax.experimental import pallas as pl
from jax.experimental.pallas import tpu as pltpu
from jax.sharding import PartitionSpec as P

HIST = 16
STEPS = 4
LANES = 128
SUBS = 8
SOFTEN = 0.25
AREA_ROW = 3
STORED_ROW = 4
SOURCE_ROWS = 24
COEFS = 4


VMEM = pl.BlockSpec(memory_space=pltpu.VMEM)
SMEM = pl.BlockSpec(memory_space=pltpu.SMEM)


def spline_coefs(rows, scale):
    d, c, b, a = rows
    return (
        (b + 4.0 * c + d) * scale,
        3.0 * (b - d) * scale,
        3.0 * (b - 2.0 * c + d) * scale,
        (a - d + 3.0 * (c - b)) * scale,
    )


def spread_targets(tgt_ref, tile, tb_ref):
    group, start = tile // 2, (tile % 2) * 2
    for k in range(3):
        for b in range(2):
            row = tgt_ref[group, pl.ds(4 * k + b + start, 1), :]
            tb_ref[k, b * LANES : (b + 1) * LANES, :] = jnp.transpose(jnp.broadcast_to(row, (LANES, LANES)), (1, 0))


def pair_sums(steps, nodes, tb_ref, geo_ref, coef_ref, acc_ref):
    def block_fn(i, carry):
        rows = pl.ds(pl.multiple_of(i * SUBS, SUBS), SUBS)
        coords = [tb_ref[k, rows, :] for k in range(3)]
        sums = [None] * steps
        for c in range(nodes // LANES):
            cols = slice(c * LANES, (c + 1) * LANES)
            dist_sq = None
            for k in range(3):
                delta = coords[k] - geo_ref[k, :, cols]
                square = delta * delta
                dist_sq = square if dist_sq is None else dist_sq + square
            weight = lax.rsqrt(dist_sq + SOFTEN)
            u = 1.0 / (1.0 + dist_sq)
            for n in range(steps):
                mix = coef_ref[n * COEFS + 3, :, cols]
                for power in (2, 1, 0):
                    mix = mix * u + coef_ref[n * COEFS + power, :, cols]
                term = weight * mix
                sums[n] = term if sums[n] is None else sums[n] + term
        for n in range(steps):
            acc_ref[n, rows, :] = sums[n]
        return carry

    lax.fori_loop(0, acc_ref.shape[1] // SUBS, block_fn, 0, unroll=acc_ref.shape[1] // SUBS)


def lane_totals(acc_ref, n):
    return [
        jnp.sum(jnp.transpose(acc_ref[n, b * LANES : (b + 1) * LANES, :], (1, 0)), axis=0, keepdims=True)
        for b in range(2)
    ]


def spread(ref, index, row):
    ref[index, :, :] = jnp.broadcast_to(row, ref.shape[1:])


def order_kernel(count_ref, lag_ref, order_ref):
    pairs = lag_ref.shape[1]
    filled = jnp.int32(0)
    for lag in range(1, STEPS):

        def pair_fn(p, filled, lag=lag):
            hit = lag_ref[0, p] == lag

            @pl.when(hit)
            def _():
                order_ref[filled] = p

            return filled + hit.astype(jnp.int32)

        filled = lax.fori_loop(0, count_ref[0], pair_fn, filled)
        order_ref[pairs + lag - 1] = filled


def two_at_a_time(count, pick, lists, tgt_ref, src_ref, works, steps, window_of, add):
    target_ref, source_ref, lag_ref = lists
    nodes = src_ref.shape[2]

    def turn_fn(turn, carry):
        tiles = []
        for side, (tb, geo, coef, acc) in enumerate(works):
            place = 2 * turn + side
            p = pick(jnp.minimum(place, count - 1))
            tile, member, lag = target_ref[0, p], source_ref[0, p], lag_ref[0, p]
            factor = jnp.where(place < count, 1.0 / 6.0, 0.0)
            spread_targets(tgt_ref, tile, tb)
            for k in range(3):
                spread(geo, k, src_ref[member, k : k + 1, :])
            scale = src_ref[member, AREA_ROW : AREA_ROW + 1, :] * factor
            window = window_of(member, lag)
            for n in range(steps):
                for power, value in enumerate(spline_coefs(window[n : n + 4], scale)):
                    spread(coef, n * COEFS + power, value)
            pair_sums(steps, nodes, tb, geo, coef, acc)
            tiles.append(tile)
        for tile, (_, _, _, acc) in zip(tiles, works):
            add(tile, jnp.concatenate([row for n in range(steps) for row in lane_totals(acc, n)], axis=0))
        return carry

    lax.fori_loop(0, (count + 1) // 2, turn_fn, 0)


def history_kernel(count_ref, target_ref, source_ref, lag_ref, tgt_ref, src_ref, out_ref, *work):
    out_ref[...] = jnp.zeros_like(out_ref)

    def window_of(member, lag):
        first = STORED_ROW + HIST - 3 - lag
        return [src_ref[member, pl.ds(first + i, 1), :] for i in range(STEPS + 3)]

    def add(tile, rows):
        out_ref[tile] += rows

    lists = (target_ref, source_ref, lag_ref)
    two_at_a_time(
        count_ref[0], lambda p: p, lists, tgt_ref, src_ref, (work[:4], work[4:]), STEPS, window_of, add
    )


def thirds(row):
    high = row.astype(jnp.bfloat16)
    rest = row - high.astype(jnp.float32)
    middle = rest.astype(jnp.bfloat16)
    low = (rest - middle.astype(jnp.float32)).astype(jnp.bfloat16)
    return jnp.concatenate([high, middle, low, jnp.zeros((13, row.shape[1]), jnp.bfloat16)], axis=0)


def one_hot_dot(row, chosen, contract):
    parts = lax.dot_general(thirds(row), chosen, (((1,), (contract,)), ((), ())), preferred_element_type=jnp.float32)
    return parts[0:1, :] + (parts[1:2, :] + parts[2:3, :])


def one_hot(index_ref, nodes):
    node = lax.broadcasted_iota(jnp.int32, (nodes, index_ref.shape[1]), 0)
    return jnp.where(node == index_ref[...], 1.0, 0.0).astype(jnp.bfloat16)


def pick_trace(density, send_ref):
    return one_hot_dot(density, one_hot(send_ref, density.shape[1]), 0)


def junction_of(trace, recv_ref, gain_ref, nodes):
    return one_hot_dot(trace * gain_ref[...], one_hot(recv_ref, nodes), 1)


def step_kernel(
    step, order_ref, target_ref, source_ref, lag_ref, place_ref, tgt_ref, src_ref, send_ref, own_ref, *refs
):
    new_refs = refs[:step]
    out_ref, new = refs[step : step + 2]
    work = refs[step + 2 :]
    nodes = src_ref.shape[2]
    region, group = place_ref[0], place_ref[2]
    out_ref[...] = jnp.zeros_like(out_ref)
    new[...] = jnp.zeros_like(new)
    for j in range(step):
        for r in range(nodes // LANES):
            new[:, 3 + j, r * LANES : (r + 1) * LANES] = new_refs[j][:, r, :]
    trace = pick_trace(own_ref[...], send_ref)
    tiles = tgt_ref.shape[0] * 2
    for other in range(out_ref.shape[0] // tiles):

        @pl.when(other != region)
        def _():
            out_ref[other * tiles + 2 * group] = jnp.concatenate([trace, trace], axis=0)

    def window_of(member, lag):
        return [new[member, pl.ds(step - lag + i, 1), :] for i in range(4)]

    def add(tile, rows):
        out_ref[region * tiles + tile] += rows

    lists = (target_ref, source_ref, lag_ref)
    count = order_ref[target_ref.shape[1] + step - 1]
    two_at_a_time(
        count, lambda p: order_ref[p], lists, tgt_ref, src_ref, (work[:4], work[4:]), 1, window_of, add
    )


def first_trace_kernel(send_ref, hist_ref, trace_ref):
    trace = pick_trace(hist_ref[HIST - 1 : HIST, :], send_ref)
    for r in range(trace_ref.shape[0]):
        trace_ref[r] = trace


def density_kernel(step, place_ref, part_ref, recv_ref, gain_ref, inc_ref, self_ref, *refs):
    nodes = inc_ref.shape[1]
    region, partner, group = place_ref[0], place_ref[1], place_ref[2]
    last = step == STEPS - 1
    if step == 0:
        trace_ref, dens_ref, row_ref, past_ref = refs
        groups = part_ref.shape[0] // 2
        fields = []
        for h in range(2):
            total = part_ref[h]
            for g in range(1, groups):
                total = total + part_ref[2 * g + h]
            fields.append(total)
        past = jnp.concatenate(fields, axis=0)
        past_ref[...] = past
        trace = trace_ref[partner]
        rows = [past[8 * h + b : 8 * h + b + 1, :] for h in range(2) for b in range(2)]
    else:
        past_ref = refs[0]
        groups = part_ref.shape[0] // 8
        first = region * (2 * groups)
        rows = []
        for h in range(2):
            total = past_ref[8 * h + 2 * step : 8 * h + 2 * step + 2, :]
            for g in range(groups):
                total = total + part_ref[first + 2 * g + h]
            rows += [total[0:1, :], total[1:2, :]]
        trace = part_ref[(partner * groups + group) * 2][0:1, :]
    field = jnp.concatenate(rows, axis=1)
    junction = junction_of(trace, recv_ref, gain_ref, nodes)
    density = (inc_ref[step : step + 1, :] - field - junction) / self_ref[...]
    if last:
        row_refs, out_ref = refs[1:-1], refs[-1]
        for n in range(STEPS - 1):
            out_ref[n : n + 1, :] = row_refs[n][...]
        out_ref[STEPS - 1 : STEPS, :] = density
    else:
        if step > 0:
            dens_ref, row_ref = refs[1:]
        row_ref[...] = density
        for r in range(nodes // LANES):
            part = density[:, r * LANES : (r + 1) * LANES]
            dens_ref[:, r, :] = jnp.broadcast_to(part, (dens_ref.shape[0], LANES))


def body(
    history,
    incident,
    positions,
    area,
    self_weight,
    pair_target,
    pair_source,
    pair_lag,
    pair_count,
    junc_send,
    junc_recv,
    junc_gain,
    adjacency,
):
    nodes = history.shape[1]
    half = nodes // 2
    jrows = junc_send.shape[1]
    groups, regions, loops = (lax.axis_size(name) for name in ("group", "region", "loop"))
    tiles = 2 * groups
    f32 = jnp.float32
    shape = jax.ShapeDtypeStruct
    region = lax.axis_index("region")
    place = jnp.stack([region, (region + adjacency[0]) % regions, lax.axis_index("group")]).astype(jnp.int32)
    self_row = self_weight.reshape(1, nodes)
    lists = (pair_count, pair_target, pair_source, pair_lag)
    line_rows = nodes // LANES

    packed = jnp.concatenate(
        [positions, area[None], history, jnp.zeros((SOURCE_ROWS - STORED_ROW - HIST, nodes), f32)], axis=0
    )
    sources = lax.all_to_all(jnp.broadcast_to(packed, (loops, SOURCE_ROWS, nodes)), "loop", 0, 0, tiled=True)
    mine = positions.reshape(3 * line_rows, LANES)
    targets = lax.all_to_all(jnp.broadcast_to(mine, (groups,) + mine.shape), "group", 0, 0, tiled=True)
    trace = pl.pallas_call(
        first_trace_kernel, out_shape=shape((regions, 1, jrows), f32), in_specs=[VMEM] * 2, out_specs=VMEM
    )(junc_send, history)
    traces = lax.all_to_all(trace, "region", 0, 0, tiled=True)
    order = pl.pallas_call(
        order_kernel,
        out_shape=shape((pair_lag.shape[1] + STEPS - 1,), jnp.int32),
        in_specs=[SMEM] * 2,
        out_specs=SMEM,
    )(pair_count, pair_lag)

    def work(steps):
        return [
            pltpu.VMEM((3, half, LANES), f32),
            pltpu.VMEM((3, SUBS, nodes), f32),
            pltpu.VMEM((steps * COEFS, SUBS, nodes), f32),
            pltpu.VMEM((steps, half, LANES), f32),
        ]

    partial_fields = pl.pallas_call(
        history_kernel,
        out_shape=shape((tiles, 2 * STEPS, LANES), f32),
        in_specs=[SMEM] * 4 + [VMEM] * 2,
        out_specs=VMEM,
        scratch_shapes=work(STEPS) * 2,
    )(*lists, targets, sources)
    parts = lax.all_to_all(partial_fields, "group", 0, 0, tiled=True)

    dens_shape, row_shape = shape((loops, line_rows, LANES), f32), shape((1, nodes), f32)
    rows, gathered = [], []
    past = None
    for step in range(STEPS):
        if step > 0:
            partial_fields = pl.pallas_call(
                functools.partial(step_kernel, step),
                out_shape=shape((regions * tiles, 2, LANES), f32),
                in_specs=[SMEM] * 5 + [VMEM] * (4 + step),
                out_specs=VMEM,
                scratch_shapes=[pltpu.VMEM((loops, SUBS, nodes), f32)] + work(1) * 2,
            )(order, *lists[1:], place, targets, sources, junc_send, rows[-1], *gathered)
            parts = lax.all_to_all(partial_fields, ("region", "group"), 0, 0, tiled=True)
        operands = [place, parts, junc_recv, junc_gain, incident, self_row]
        if step == 0:
            operands += [traces]
            out_shape = [dens_shape, row_shape, shape((2 * 2 * STEPS, LANES), f32)]
        elif step < STEPS - 1:
            operands += [past]
            out_shape = [dens_shape, row_shape]
        else:
            operands += [past] + rows
            out_shape = [shape((STEPS, nodes), f32)]
        results = pl.pallas_call(
            functools.partial(density_kernel, step),
            out_shape=out_shape,
            in_specs=[SMEM] + [VMEM] * (len(operands) - 1),
            out_specs=[VMEM] * len(out_shape),
        )(*operands)
        if step == 0:
            past = results[2]
        if step < STEPS - 1:
            rows.append(results[1])
            gathered.append(lax.all_to_all(results[0], "loop", 0, 0, tiled=True))
    return results[0]


def solution(mesh):
    blocks = ("region", "group", "loop")
    in_specs = (
        P(None, blocks),
        P(None, blocks),
        P(None, blocks),
        P(blocks),
        P(blocks),
        P(blocks, None),
        P(blocks, None),
        P(blocks, None),
        P(blocks),
        P(blocks, None),
        P(blocks, None),
        P(blocks, None),
        P(blocks),
    )
    return jax.shard_map(body, mesh=mesh, in_specs=in_specs, out_specs=P(None, blocks), check_vma=False)
```

```python
import functools

import jax
import jax.numpy as jnp
from jax import lax
from jax.experimental import pallas as pl
from jax.experimental.pallas import tpu as pltpu
from jax.sharding import PartitionSpec as P

HIST = 16
STEPS = 4
LANES = 128
SUBS = 8
SOFTEN = 0.25
AREA_ROW = 3
STORED_ROW = 4
SOURCE_ROWS = 24
COEFS = 4


PAIR_GRANT = pltpu.CompilerParams(vmem_limit_bytes=12 * 2**20)
SMALL_GRANT = pltpu.CompilerParams(vmem_limit_bytes=4 * 2**20)
VMEM = pl.BlockSpec(memory_space=pltpu.VMEM)
SMEM = pl.BlockSpec(memory_space=pltpu.SMEM)


def spline_coefs(rows, scale):
    d, c, b, a = rows
    return (
        (b + 4.0 * c + d) * scale,
        3.0 * (b - d) * scale,
        3.0 * (b - 2.0 * c + d) * scale,
        (a - d + 3.0 * (c - b)) * scale,
    )


def spread_targets(tgt_ref, tile, tb_ref):
    group, start = tile // 2, (tile % 2) * 2
    for k in range(3):
        for b in range(2):
            row = tgt_ref[group, pl.ds(4 * k + b + start, 1), :]
            tb_ref[k, b * LANES : (b + 1) * LANES, :] = jnp.transpose(jnp.broadcast_to(row, (LANES, LANES)), (1, 0))


def pair_sums(steps, nodes, tb_ref, geo_ref, coef_ref, acc_ref):
    def block_fn(i, carry):
        rows = pl.ds(pl.multiple_of(i * SUBS, SUBS), SUBS)
        coords = [tb_ref[k, rows, :] for k in range(3)]
        sums = [None] * steps
        for c in range(nodes // LANES):
            cols = slice(c * LANES, (c + 1) * LANES)
            dist_sq = None
            for k in range(3):
                delta = coords[k] - geo_ref[k, :, cols]
                square = delta * delta
                dist_sq = square if dist_sq is None else dist_sq + square
            weight = lax.rsqrt(dist_sq + SOFTEN)
            u = 1.0 / (1.0 + dist_sq)
            for n in range(steps):
                mix = coef_ref[n * COEFS + 3, :, cols]
                for power in (2, 1, 0):
                    mix = mix * u + coef_ref[n * COEFS + power, :, cols]
                term = weight * mix
                sums[n] = term if sums[n] is None else sums[n] + term
        for n in range(steps):
            acc_ref[n, rows, :] = sums[n]
        return carry

    lax.fori_loop(0, acc_ref.shape[1] // SUBS, block_fn, 0, unroll=acc_ref.shape[1] // SUBS)


def lane_totals(acc_ref, n):
    return [
        jnp.sum(jnp.transpose(acc_ref[n, b * LANES : (b + 1) * LANES, :], (1, 0)), axis=0, keepdims=True)
        for b in range(2)
    ]


def spread(ref, index, row):
    ref[index, :, :] = jnp.broadcast_to(row, ref.shape[1:])


def order_kernel(count_ref, lag_ref, order_ref):
    pairs = lag_ref.shape[1]
    filled = jnp.int32(0)
    for lag in range(1, STEPS):

        def pair_fn(p, filled, lag=lag):
            hit = lag_ref[0, p] == lag

            @pl.when(hit)
            def _():
                order_ref[filled] = p

            return filled + hit.astype(jnp.int32)

        filled = lax.fori_loop(0, count_ref[0], pair_fn, filled)
        order_ref[pairs + lag - 1] = filled


def two_at_a_time(count, pick, lists, tgt_ref, src_ref, works, steps, window_of, add):
    target_ref, source_ref, lag_ref = lists
    nodes = src_ref.shape[2]

    def turn_fn(turn, carry):
        tiles = []
        for side, (tb, geo, coef, acc) in enumerate(works):
            place = 2 * turn + side
            p = pick(jnp.minimum(place, count - 1))
            tile, member, lag = target_ref[0, p], source_ref[0, p], lag_ref[0, p]
            factor = jnp.where(place < count, 1.0 / 6.0, 0.0)
            spread_targets(tgt_ref, tile, tb)
            for k in range(3):
                spread(geo, k, src_ref[member, k : k + 1, :])
            scale = src_ref[member, AREA_ROW : AREA_ROW + 1, :] * factor
            window = window_of(member, lag)
            for n in range(steps):
                for power, value in enumerate(spline_coefs(window[n : n + 4], scale)):
                    spread(coef, n * COEFS + power, value)
            pair_sums(steps, nodes, tb, geo, coef, acc)
            tiles.append(tile)
        for tile, (_, _, _, acc) in zip(tiles, works):
            add(tile, jnp.concatenate([row for n in range(steps) for row in lane_totals(acc, n)], axis=0))
        return carry

    lax.fori_loop(0, (count + 1) // 2, turn_fn, 0)


def history_kernel(count_ref, target_ref, source_ref, lag_ref, tgt_ref, src_ref, out_ref, *work):
    out_ref[...] = jnp.zeros_like(out_ref)

    def window_of(member, lag):
        first = STORED_ROW + HIST - 3 - lag
        return [src_ref[member, pl.ds(first + i, 1), :] for i in range(STEPS + 3)]

    def add(tile, rows):
        out_ref[tile] += rows

    lists = (target_ref, source_ref, lag_ref)
    two_at_a_time(
        count_ref[0], lambda p: p, lists, tgt_ref, src_ref, (work[:4], work[4:]), STEPS, window_of, add
    )


def thirds(row):
    high = row.astype(jnp.bfloat16)
    rest = row - high.astype(jnp.float32)
    middle = rest.astype(jnp.bfloat16)
    low = (rest - middle.astype(jnp.float32)).astype(jnp.bfloat16)
    return jnp.concatenate([high, middle, low, jnp.zeros((13, row.shape[1]), jnp.bfloat16)], axis=0)


def one_hot_dot(row, chosen, contract):
    parts = lax.dot_general(thirds(row), chosen, (((1,), (contract,)), ((), ())), preferred_element_type=jnp.float32)
    return parts[0:1, :] + (parts[1:2, :] + parts[2:3, :])


def one_hot(index_ref, nodes):
    node = lax.broadcasted_iota(jnp.int32, (nodes, index_ref.shape[1]), 0)
    return jnp.where(node == index_ref[...], 1.0, 0.0).astype(jnp.bfloat16)


def pick_trace(density, send_ref):
    return one_hot_dot(density, one_hot(send_ref, density.shape[1]), 0)


def junction_of(trace, recv_ref, gain_ref, nodes):
    return one_hot_dot(trace * gain_ref[...], one_hot(recv_ref, nodes), 1)


def step_kernel(
    step, order_ref, target_ref, source_ref, lag_ref, place_ref, tgt_ref, src_ref, send_ref, own_ref, *refs
):
    new_refs = refs[:step]
    out_ref, new = refs[step : step + 2]
    work = refs[step + 2 :]
    nodes = src_ref.shape[2]
    region, group = place_ref[0], place_ref[2]
    out_ref[...] = jnp.zeros_like(out_ref)
    new[...] = jnp.zeros_like(new)
    for j in range(step):
        for r in range(nodes // LANES):
            new[:, 3 + j, r * LANES : (r + 1) * LANES] = new_refs[j][:, r, :]
    trace = pick_trace(own_ref[...], send_ref)
    tiles = tgt_ref.shape[0] * 2
    for other in range(out_ref.shape[0] // tiles):

        @pl.when(other != region)
        def _():
            out_ref[other * tiles + 2 * group] = jnp.concatenate([trace, trace], axis=0)

    def window_of(member, lag):
        return [new[member, pl.ds(step - lag + i, 1), :] for i in range(4)]

    def add(tile, rows):
        out_ref[region * tiles + tile] += rows

    lists = (target_ref, source_ref, lag_ref)
    count = order_ref[target_ref.shape[1] + step - 1]
    two_at_a_time(
        count, lambda p: order_ref[p], lists, tgt_ref, src_ref, (work[:4], work[4:]), 1, window_of, add
    )


def first_trace_kernel(send_ref, hist_ref, trace_ref):
    trace = pick_trace(hist_ref[HIST - 1 : HIST, :], send_ref)
    for r in range(trace_ref.shape[0]):
        trace_ref[r] = trace


def density_kernel(step, place_ref, part_ref, recv_ref, gain_ref, inc_ref, self_ref, *refs):
    nodes = inc_ref.shape[1]
    region, partner, group = place_ref[0], place_ref[1], place_ref[2]
    last = step == STEPS - 1
    if step == 0:
        trace_ref, dens_ref, row_ref, past_ref = refs
        groups = part_ref.shape[0] // 2
        fields = []
        for h in range(2):
            total = part_ref[h]
            for g in range(1, groups):
                total = total + part_ref[2 * g + h]
            fields.append(total)
        past = jnp.concatenate(fields, axis=0)
        past_ref[...] = past
        trace = trace_ref[partner]
        rows = [past[8 * h + b : 8 * h + b + 1, :] for h in range(2) for b in range(2)]
    else:
        past_ref = refs[0]
        groups = part_ref.shape[0] // 8
        first = region * (2 * groups)
        rows = []
        for h in range(2):
            total = past_ref[8 * h + 2 * step : 8 * h + 2 * step + 2, :]
            for g in range(groups):
                total = total + part_ref[first + 2 * g + h]
            rows += [total[0:1, :], total[1:2, :]]
        trace = part_ref[(partner * groups + group) * 2][0:1, :]
    field = jnp.concatenate(rows, axis=1)
    junction = junction_of(trace, recv_ref, gain_ref, nodes)
    density = (inc_ref[step : step + 1, :] - field - junction) / self_ref[...]
    if last:
        row_refs, out_ref = refs[1:-1], refs[-1]
        for n in range(STEPS - 1):
            out_ref[n : n + 1, :] = row_refs[n][...]
        out_ref[STEPS - 1 : STEPS, :] = density
    else:
        if step > 0:
            dens_ref, row_ref = refs[1:]
        row_ref[...] = density
        for r in range(nodes // LANES):
            part = density[:, r * LANES : (r + 1) * LANES]
            dens_ref[:, r, :] = jnp.broadcast_to(part, (dens_ref.shape[0], LANES))


def body(
    history,
    incident,
    positions,
    area,
    self_weight,
    pair_target,
    pair_source,
    pair_lag,
    pair_count,
    junc_send,
    junc_recv,
    junc_gain,
    adjacency,
):
    nodes = history.shape[1]
    half = nodes // 2
    jrows = junc_send.shape[1]
    groups, regions, loops = (lax.axis_size(name) for name in ("group", "region", "loop"))
    tiles = 2 * groups
    f32 = jnp.float32
    shape = jax.ShapeDtypeStruct
    region = lax.axis_index("region")
    place = jnp.stack([region, (region + adjacency[0]) % regions, lax.axis_index("group")]).astype(jnp.int32)
    self_row = self_weight.reshape(1, nodes)
    lists = (pair_count, pair_target, pair_source, pair_lag)
    line_rows = nodes // LANES

    packed = jnp.concatenate(
        [positions, area[None], history, jnp.zeros((SOURCE_ROWS - STORED_ROW - HIST, nodes), f32)], axis=0
    )
    sources = lax.all_to_all(jnp.broadcast_to(packed, (loops, SOURCE_ROWS, nodes)), "loop", 0, 0, tiled=True)
    mine = positions.reshape(3 * line_rows, LANES)
    targets = lax.all_to_all(jnp.broadcast_to(mine, (groups,) + mine.shape), "group", 0, 0, tiled=True)
    trace = pl.pallas_call(
        first_trace_kernel,
        out_shape=shape((regions, 1, jrows), f32),
        in_specs=[VMEM] * 2,
        out_specs=VMEM,
        compiler_params=SMALL_GRANT,
    )(junc_send, history)
    traces = lax.all_to_all(trace, "region", 0, 0, tiled=True)
    order = pl.pallas_call(
        order_kernel,
        out_shape=shape((pair_lag.shape[1] + STEPS - 1,), jnp.int32),
        in_specs=[SMEM] * 2,
        out_specs=SMEM,
        compiler_params=SMALL_GRANT,
    )(pair_count, pair_lag)

    def work(steps):
        return [
            pltpu.VMEM((3, half, LANES), f32),
            pltpu.VMEM((3, SUBS, nodes), f32),
            pltpu.VMEM((steps * COEFS, SUBS, nodes), f32),
            pltpu.VMEM((steps, half, LANES), f32),
        ]

    partial_fields = pl.pallas_call(
        history_kernel,
        out_shape=shape((tiles, 2 * STEPS, LANES), f32),
        in_specs=[SMEM] * 4 + [VMEM] * 2,
        out_specs=VMEM,
        scratch_shapes=work(STEPS) * 2,
        compiler_params=PAIR_GRANT,
    )(*lists, targets, sources)
    parts = lax.all_to_all(partial_fields, "group", 0, 0, tiled=True)

    dens_shape, row_shape = shape((loops, line_rows, LANES), f32), shape((1, nodes), f32)
    rows, gathered = [], []
    past = None
    for step in range(STEPS):
        if step > 0:
            partial_fields = pl.pallas_call(
                functools.partial(step_kernel, step),
                out_shape=shape((regions * tiles, 2, LANES), f32),
                in_specs=[SMEM] * 5 + [VMEM] * (4 + step),
                out_specs=VMEM,
                scratch_shapes=[pltpu.VMEM((loops, SUBS, nodes), f32)] + work(1) * 2,
                compiler_params=PAIR_GRANT,
            )(order, *lists[1:], place, targets, sources, junc_send, rows[-1], *gathered)
            parts = lax.all_to_all(partial_fields, ("region", "group"), 0, 0, tiled=True)
        operands = [place, parts, junc_recv, junc_gain, incident, self_row]
        if step == 0:
            operands += [traces]
            out_shape = [dens_shape, row_shape, shape((2 * 2 * STEPS, LANES), f32)]
        elif step < STEPS - 1:
            operands += [past]
            out_shape = [dens_shape, row_shape]
        else:
            operands += [past] + rows
            out_shape = [shape((STEPS, nodes), f32)]
        results = pl.pallas_call(
            functools.partial(density_kernel, step),
            out_shape=out_shape,
            in_specs=[SMEM] + [VMEM] * (len(operands) - 1),
            out_specs=[VMEM] * len(out_shape),
            compiler_params=SMALL_GRANT,
        )(*operands)
        if step == 0:
            past = results[2]
        if step < STEPS - 1:
            rows.append(results[1])
            gathered.append(lax.all_to_all(results[0], "loop", 0, 0, tiled=True))
    return results[0]


def solution(mesh):
    blocks = ("region", "group", "loop")
    in_specs = (
        P(None, blocks),
        P(None, blocks),
        P(None, blocks),
        P(blocks),
        P(blocks),
        P(blocks, None),
        P(blocks, None),
        P(blocks, None),
        P(blocks),
        P(blocks, None),
        P(blocks, None),
        P(blocks, None),
        P(blocks),
    )
    return jax.shard_map(body, mesh=mesh, in_specs=in_specs, out_specs=P(None, blocks), check_vma=False)
```

```python
import functools

import jax
import jax.numpy as jnp
from jax import lax
from jax.experimental import pallas as pl
from jax.experimental.pallas import tpu as pltpu
from jax.sharding import PartitionSpec as P


HIST = 16
STEPS = 4
LANES = 128
SUBS = 8
SOFTEN = 0.25
AREA_ROW = 3
STORED_ROW = 4
FIRST_STORED = 1
COEFS = 4


PAIR_GRANT = pltpu.CompilerParams(vmem_limit_bytes=12 * 2**20)
SMALL_GRANT = pltpu.CompilerParams(vmem_limit_bytes=4 * 2**20)
VMEM = pl.BlockSpec(memory_space=pltpu.VMEM)
SMEM = pl.BlockSpec(memory_space=pltpu.SMEM)


def spline_coefs(rows, scale):
    d, c, b, a = rows
    return (
        (b + 4.0 * c + d) * scale,
        3.0 * (b - d) * scale,
        3.0 * (b - 2.0 * c + d) * scale,
        (a - d + 3.0 * (c - b)) * scale,
    )


def spread_targets(tgt_ref, tile, tb_ref):
    group, start = tile // 2, (tile % 2) * (2 * LANES)
    for k in range(3):
        for b in range(2):
            row = tgt_ref[group, k : k + 1, pl.ds(pl.multiple_of(start + b * LANES, LANES), LANES)]
            tb_ref[k, b * LANES : (b + 1) * LANES, :] = jnp.transpose(jnp.broadcast_to(row, (LANES, LANES)), (1, 0))


def pair_sums(steps, nodes, tb_ref, geo_ref, coef_ref, acc_ref):
    def block_fn(i, carry):
        rows = pl.ds(pl.multiple_of(i * SUBS, SUBS), SUBS)
        coords = [tb_ref[k, rows, :] for k in range(3)]
        sums = [None] * steps
        for c in range(nodes // LANES):
            cols = slice(c * LANES, (c + 1) * LANES)
            dist_sq = None
            for k in range(3):
                delta = coords[k] - geo_ref[k, :, cols]
                square = delta * delta
                dist_sq = square if dist_sq is None else dist_sq + square
            weight = lax.rsqrt(dist_sq + SOFTEN)
            u = 1.0 / (1.0 + dist_sq)
            for n in range(steps):
                mix = coef_ref[n * COEFS + 3, :, cols]
                for power in (2, 1, 0):
                    mix = mix * u + coef_ref[n * COEFS + power, :, cols]
                term = weight * mix
                sums[n] = term if sums[n] is None else sums[n] + term
        for n in range(steps):
            acc_ref[n, rows, :] = sums[n]
        return carry

    lax.fori_loop(0, acc_ref.shape[1] // SUBS, block_fn, 0, unroll=acc_ref.shape[1] // SUBS)


def lane_totals(acc_ref, n):
    return [
        jnp.sum(jnp.transpose(acc_ref[n, b * LANES : (b + 1) * LANES, :], (1, 0)), axis=0, keepdims=True)
        for b in range(2)
    ]


def spread(ref, index, lines):
    for c in range(lines.shape[0]):
        ref[index, :, c * LANES : (c + 1) * LANES] = jnp.broadcast_to(lines[c : c + 1, :], (SUBS, LANES))


def order_kernel(count_ref, lag_ref, order_ref):
    pairs, count = lag_ref.shape[1], count_ref[0]
    lags = [jnp.where(p < count, lag_ref[0, p], 0) for p in range(pairs)]
    filled = jnp.int32(0)
    ends = []
    for lag in range(1, STEPS):
        for p in range(pairs):
            order_ref[filled] = p
            filled = filled + (lags[p] == lag).astype(jnp.int32)
        ends.append(filled)
    for place, end in enumerate(ends + [count]):
        order_ref[pairs + place] = end


def two_at_a_time(count, pick, lists, tgt_ref, src_ref, works, steps, window_of, add):
    target_ref, source_ref, lag_ref = lists
    nodes = src_ref.shape[2] * LANES

    def turn_fn(turn, carry):
        tiles = []
        for side, (tb, geo, coef, acc) in enumerate(works):
            place = 2 * turn + side
            p = pick(jnp.minimum(place, count - 1))
            tile, member, lag = target_ref[0, p], source_ref[0, p], lag_ref[0, p]
            factor = jnp.where(place < count, 1.0 / 6.0, 0.0)
            spread_targets(tgt_ref, tile, tb)
            for k in range(3):
                spread(geo, k, src_ref[member, k])
            scale = src_ref[member, AREA_ROW] * factor
            window = window_of(member, lag)
            for n in range(steps):
                for power, value in enumerate(spline_coefs(window[n : n + 4], scale)):
                    spread(coef, n * COEFS + power, value)
            pair_sums(steps, nodes, tb, geo, coef, acc)
            tiles.append(tile)
        for tile, (_, _, _, acc) in zip(tiles, works):
            add(tile, jnp.concatenate([row for n in range(steps) for row in lane_totals(acc, n)], axis=0))
        return carry

    lax.fori_loop(0, (count + 1) // 2, turn_fn, 0)


def history_kernel(order_ref, target_ref, source_ref, lag_ref, tgt_ref, src_ref, out_ref, *work):
    out_ref[...] = jnp.zeros_like(out_ref)

    def window_of(member, lag):
        first, end = STORED_ROW - FIRST_STORED + HIST - 3 - lag, src_ref.shape[1]
        rows = [src_ref[member, first + i] for i in range(4)]
        for i in range(4, STEPS + 3):
            row = src_ref[member, jnp.minimum(first + i, end - 1)]
            rows.append(jnp.where(first + i < end, row, 0.0))
        return rows

    def add(tile, rows):
        out_ref[tile] += rows

    lists = (target_ref, source_ref, lag_ref)
    two_at_a_time(
        order_ref[target_ref.shape[1] + STEPS - 1], lambda p: p, lists, tgt_ref, src_ref, (work[:4], work[4:]), STEPS, window_of, add
    )


def thirds(row):
    high = row.astype(jnp.bfloat16)
    rest = row - high.astype(jnp.float32)
    middle = rest.astype(jnp.bfloat16)
    low = (rest - middle.astype(jnp.float32)).astype(jnp.bfloat16)
    return jnp.concatenate([high, middle, low, jnp.zeros((13, row.shape[1]), jnp.bfloat16)], axis=0)


def one_hot_dot(row, chosen, contract):
    parts = lax.dot_general(thirds(row), chosen, (((1,), (contract,)), ((), ())), preferred_element_type=jnp.float32)
    return parts[0:1, :] + (parts[1:2, :] + parts[2:3, :])


def one_hot(index_ref, nodes):
    node = lax.broadcasted_iota(jnp.int32, (nodes, index_ref.shape[1]), 0)
    return jnp.where(node == index_ref[...], 1.0, 0.0).astype(jnp.bfloat16)


def pick_trace(density, send_ref):
    return one_hot_dot(density, one_hot(send_ref, density.shape[1]), 0)


def junction_of(trace, recv_ref, gain_ref, nodes):
    return one_hot_dot(trace * gain_ref[...], one_hot(recv_ref, nodes), 1)


def step_kernel(
    step, order_ref, target_ref, source_ref, lag_ref, place_ref, tgt_ref, src_ref, send_ref, own_ref, *refs
):
    new_refs = refs[:step]
    out_ref, new = refs[step : step + 2]
    work = refs[step + 2 :]
    region, group = place_ref[0], place_ref[2]
    out_ref[...] = jnp.zeros_like(out_ref)
    new[...] = jnp.zeros_like(new)
    for j in range(step):
        new[:, 3 + j] = new_refs[j][...]
    trace = pick_trace(own_ref[...], send_ref)
    tiles = tgt_ref.shape[0] * 2
    for other in range(out_ref.shape[0] // tiles):

        @pl.when(other != region)
        def _():
            out_ref[other * tiles + 2 * group] = jnp.concatenate([trace, trace], axis=0)

    def window_of(member, lag):
        return [new[member, step - lag + i] for i in range(4)]

    def add(tile, rows):
        out_ref[region * tiles + tile] += rows

    lists = (target_ref, source_ref, lag_ref)
    count = order_ref[target_ref.shape[1] + step - 1]
    two_at_a_time(
        count, lambda p: order_ref[p], lists, tgt_ref, src_ref, (work[:4], work[4:]), 1, window_of, add
    )


def first_trace_kernel(send_ref, hist_ref, trace_ref):
    trace = pick_trace(hist_ref[HIST - 1 : HIST, :], send_ref)
    for r in range(trace_ref.shape[0]):
        trace_ref[r] = trace


def density_kernel(step, place_ref, part_ref, recv_ref, gain_ref, inc_ref, self_ref, *refs):
    nodes = inc_ref.shape[1]
    region, partner, group = place_ref[0], place_ref[1], place_ref[2]
    last = step == STEPS - 1
    if step == 0:
        trace_ref, dens_ref, row_ref, past_ref = refs
        groups = part_ref.shape[0] // 2
        fields = []
        for h in range(2):
            total = part_ref[h]
            for g in range(1, groups):
                total = total + part_ref[2 * g + h]
            fields.append(total)
        past = jnp.concatenate(fields, axis=0)
        past_ref[...] = past
        trace = trace_ref[partner]
        rows = [past[8 * h + b : 8 * h + b + 1, :] for h in range(2) for b in range(2)]
    else:
        past_ref = refs[0]
        groups = part_ref.shape[0] // 8
        first = region * (2 * groups)
        rows = []
        for h in range(2):
            total = past_ref[8 * h + 2 * step : 8 * h + 2 * step + 2, :]
            for g in range(groups):
                total = total + part_ref[first + 2 * g + h]
            rows += [total[0:1, :], total[1:2, :]]
        trace = part_ref[(partner * groups + group) * 2][0:1, :]
    field = jnp.concatenate(rows, axis=1)
    junction = junction_of(trace, recv_ref, gain_ref, nodes)
    density = (inc_ref[step : step + 1, :] - field - junction) / self_ref[...]
    if last:
        row_refs, out_ref = refs[1:-1], refs[-1]
        for n in range(STEPS - 1):
            out_ref[n : n + 1, :] = row_refs[n][...]
        out_ref[STEPS - 1 : STEPS, :] = density
    else:
        if step > 0:
            dens_ref, row_ref = refs[1:]
        row_ref[...] = density
        for r in range(nodes // LANES):
            part = density[:, r * LANES : (r + 1) * LANES]
            dens_ref[:, r, :] = jnp.broadcast_to(part, (dens_ref.shape[0], LANES))


def body(
    history,
    incident,
    positions,
    area,
    self_weight,
    pair_target,
    pair_source,
    pair_lag,
    pair_count,
    junc_send,
    junc_recv,
    junc_gain,
    adjacency,
):
    nodes = history.shape[1]
    half = nodes // 2
    jrows = junc_send.shape[1]
    groups, regions, loops = (lax.axis_size(name) for name in ("group", "region", "loop"))
    tiles = 2 * groups
    f32 = jnp.float32
    shape = jax.ShapeDtypeStruct
    region = lax.axis_index("region")
    place = jnp.stack([region, (region + adjacency[0]) % regions, lax.axis_index("group")]).astype(jnp.int32)
    self_row = self_weight.reshape(1, nodes)
    lists = (pair_target, pair_source, pair_lag)
    line_rows = nodes // LANES

    packed = jnp.concatenate([positions, area[None], history[FIRST_STORED:]], axis=0)
    packed = packed.reshape(packed.shape[0], line_rows, LANES)
    packed = jnp.broadcast_to(packed, (loops,) + packed.shape)
    sources = lax.all_to_all(packed, "loop", 0, 0, tiled=True)
    targets = lax.all_to_all(jnp.broadcast_to(positions, (groups, 3, nodes)), "group", 0, 0, tiled=True)
    order = pl.pallas_call(
        order_kernel,
        out_shape=shape((pair_lag.shape[1] + STEPS,), jnp.int32),
        in_specs=[SMEM] * 2,
        out_specs=SMEM,
        compiler_params=SMALL_GRANT,
    )(pair_count, pair_lag)
    trace = pl.pallas_call(
        first_trace_kernel,
        out_shape=shape((regions, 1, jrows), f32),
        in_specs=[VMEM] * 2,
        out_specs=VMEM,
        compiler_params=SMALL_GRANT,
    )(junc_send, history)
    traces = lax.all_to_all(trace, "region", 0, 0, tiled=True)

    def work(steps):
        return [
            pltpu.VMEM((3, half, LANES), f32),
            pltpu.VMEM((3, SUBS, nodes), f32),
            pltpu.VMEM((steps * COEFS, SUBS, nodes), f32),
            pltpu.VMEM((steps, half, LANES), f32),
        ]

    partial_fields = pl.pallas_call(
        history_kernel,
        out_shape=shape((tiles, 2 * STEPS, LANES), f32),
        in_specs=[SMEM] * 4 + [VMEM] * 2,
        out_specs=VMEM,
        scratch_shapes=work(STEPS) * 2,
        compiler_params=PAIR_GRANT,
    )(order, *lists, targets, sources)
    parts = lax.all_to_all(partial_fields, "group", 0, 0, tiled=True)

    dens_shape, row_shape = shape((loops, line_rows, LANES), f32), shape((1, nodes), f32)
    rows, gathered = [], []
    past = None
    for step in range(STEPS):
        if step > 0:
            partial_fields = pl.pallas_call(
                functools.partial(step_kernel, step),
                out_shape=shape((regions * tiles, 2, LANES), f32),
                in_specs=[SMEM] * 5 + [VMEM] * (4 + step),
                out_specs=VMEM,
                scratch_shapes=[pltpu.VMEM((loops, SUBS, line_rows, LANES), f32)] + work(1) * 2,
                compiler_params=PAIR_GRANT,
            )(order, *lists, place, targets, sources, junc_send, rows[-1], *gathered)
            parts = lax.all_to_all(partial_fields, ("region", "group"), 0, 0, tiled=True)
        operands = [place, parts, junc_recv, junc_gain, incident, self_row]
        if step == 0:
            operands += [traces]
            out_shape = [dens_shape, row_shape, shape((2 * 2 * STEPS, LANES), f32)]
        elif step < STEPS - 1:
            operands += [past]
            out_shape = [dens_shape, row_shape]
        else:
            operands += [past] + rows
            out_shape = [shape((STEPS, nodes), f32)]
        results = pl.pallas_call(
            functools.partial(density_kernel, step),
            out_shape=out_shape,
            in_specs=[SMEM] + [VMEM] * (len(operands) - 1),
            out_specs=[VMEM] * len(out_shape),
            compiler_params=SMALL_GRANT,
        )(*operands)
        if step == 0:
            past = results[2]
        if step < STEPS - 1:
            rows.append(results[1])
            gathered.append(lax.all_to_all(results[0], "loop", 0, 0, tiled=True))
    return results[0]


def solution(mesh):
    blocks = ("region", "group", "loop")
    in_specs = (
        P(None, blocks),
        P(None, blocks),
        P(None, blocks),
        P(blocks),
        P(blocks),
        P(blocks, None),
        P(blocks, None),
        P(blocks, None),
        P(blocks),
        P(blocks, None),
        P(blocks, None),
        P(blocks, None),
        P(blocks),
    )
    return jax.shard_map(body, mesh=mesh, in_specs=in_specs, out_specs=P(None, blocks), check_vma=False)
```

```python
import functools

import jax
import jax.numpy as jnp
from jax import lax
from jax.experimental import pallas as pl
from jax.experimental.pallas import tpu as pltpu
from jax.sharding import PartitionSpec as P


HIST = 16
STEPS = 4
LANES = 128
SUBS = 8
SOFTEN = 0.25
AREA_ROW = 3
STORED_ROW = 4
FIRST_STORED = 1
COEFS = 4
NEAR = 12
NEAR_COEFS = STEPS - 1


PAIR_GRANT = pltpu.CompilerParams(vmem_limit_bytes=12 * 2**20)
NEAR_GRANT = pltpu.CompilerParams(vmem_limit_bytes=12 * 2**20)
SMALL_GRANT = pltpu.CompilerParams(vmem_limit_bytes=4 * 2**20)
VMEM = pl.BlockSpec(memory_space=pltpu.VMEM)
SMEM = pl.BlockSpec(memory_space=pltpu.SMEM)


def spline_coefs(rows, scale):
    d, c, b, a = rows
    return (
        (b + 4.0 * c + d) * scale,
        3.0 * (b - d) * scale,
        3.0 * (b - 2.0 * c + d) * scale,
        (a - d + 3.0 * (c - b)) * scale,
    )


def spread_targets(tgt_ref, tile, tb_ref):
    group, start = tile // 2, (tile % 2) * (2 * LANES)
    for k in range(3):
        for b in range(2):
            row = tgt_ref[group, k : k + 1, pl.ds(pl.multiple_of(start + b * LANES, LANES), LANES)]
            tb_ref[k, b * LANES : (b + 1) * LANES, :] = jnp.transpose(jnp.broadcast_to(row, (LANES, LANES)), (1, 0))


def pair_sums(steps, nodes, tb_ref, geo_ref, coef_ref, acc_ref):
    def block_fn(i, carry):
        rows = pl.ds(pl.multiple_of(i * SUBS, SUBS), SUBS)
        coords = [tb_ref[k, rows, :] for k in range(3)]
        sums = [None] * steps
        for c in range(nodes // LANES):
            cols = slice(c * LANES, (c + 1) * LANES)
            dist_sq = None
            for k in range(3):
                delta = coords[k] - geo_ref[k, :, cols]
                square = delta * delta
                dist_sq = square if dist_sq is None else dist_sq + square
            weight = lax.rsqrt(dist_sq + SOFTEN)
            u = 1.0 / (1.0 + dist_sq)
            for n in range(steps):
                mix = coef_ref[n * COEFS + 3, :, cols]
                for power in (2, 1, 0):
                    mix = mix * u + coef_ref[n * COEFS + power, :, cols]
                term = weight * mix
                sums[n] = term if sums[n] is None else sums[n] + term
        for n in range(steps):
            acc_ref[n, rows, :] = sums[n]
        return carry

    lax.fori_loop(0, acc_ref.shape[1] // SUBS, block_fn, 0, unroll=acc_ref.shape[1] // SUBS)


def lane_totals(acc_ref, n):
    return [
        jnp.sum(jnp.transpose(acc_ref[n, b * LANES : (b + 1) * LANES, :], (1, 0)), axis=0, keepdims=True)
        for b in range(2)
    ]


def spread(ref, index, lines):
    for c in range(lines.shape[0]):
        ref[index, :, c * LANES : (c + 1) * LANES] = jnp.broadcast_to(lines[c : c + 1, :], (SUBS, LANES))


def order_kernel(count_ref, lag_ref, order_ref):
    pairs, count = lag_ref.shape[1], count_ref[0]
    lags = [jnp.where(p < count, lag_ref[0, p], 0) for p in range(pairs)]
    filled = jnp.int32(0)
    ends = []
    for lag in range(1, STEPS):
        for p in range(pairs):
            order_ref[filled] = p
            filled = filled + (lags[p] == lag).astype(jnp.int32)
        ends.append(filled)
    for place, end in enumerate(ends + [count]):
        order_ref[pairs + place] = end


def two_at_a_time(count, pick, lists, tgt_ref, src_ref, works, steps, window_of, add):
    target_ref, source_ref, lag_ref = lists
    nodes = src_ref.shape[2] * LANES

    def turn_fn(turn, carry):
        tiles = []
        for side, (tb, geo, coef, acc) in enumerate(works):
            place = 2 * turn + side
            p = pick(jnp.minimum(place, count - 1))
            tile, member, lag = target_ref[0, p], source_ref[0, p], lag_ref[0, p]
            factor = jnp.where(place < count, 1.0 / 6.0, 0.0)
            spread_targets(tgt_ref, tile, tb)
            for k in range(3):
                spread(geo, k, src_ref[member, k])
            scale = src_ref[member, AREA_ROW] * factor
            window = window_of(member, lag)
            for n in range(steps):
                for power, value in enumerate(spline_coefs(window[n : n + 4], scale)):
                    spread(coef, n * COEFS + power, value)
            pair_sums(steps, nodes, tb, geo, coef, acc)
            tiles.append(tile)
        for tile, (_, _, _, acc) in zip(tiles, works):
            add(tile, jnp.concatenate([row for n in range(steps) for row in lane_totals(acc, n)], axis=0))
        return carry

    lax.fori_loop(0, (count + 1) // 2, turn_fn, 0)


def history_kernel(order_ref, target_ref, source_ref, lag_ref, tgt_ref, src_ref, out_ref, *work):
    out_ref[...] = jnp.zeros_like(out_ref)

    def window_of(member, lag):
        first, end = STORED_ROW - FIRST_STORED + HIST - 3 - lag, src_ref.shape[1]
        rows = [src_ref[member, first + i] for i in range(4)]
        for i in range(4, STEPS + 3):
            row = src_ref[member, jnp.minimum(first + i, end - 1)]
            rows.append(jnp.where(first + i < end, row, 0.0))
        return rows

    def add(tile, rows):
        out_ref[tile] += rows

    lists = (target_ref, source_ref, lag_ref)
    two_at_a_time(
        order_ref[target_ref.shape[1] + STEPS - 1], lambda p: p, lists, tgt_ref, src_ref, (work[:4], work[4:]), STEPS, window_of, add
    )


def near_kernel(order_ref, target_ref, source_ref, tgt_ref, src_ref, near_ref, *work):
    lines = src_ref.shape[2]
    count = jnp.minimum(order_ref[target_ref.shape[1] + STEPS - 2], NEAR)
    spaces = (work[:2], work[2:])

    def turn_fn(turn, carry):
        for side, (tb, geo) in enumerate(spaces):
            slot = jnp.minimum(2 * turn + side, count - 1)
            p = order_ref[slot]
            tile, member = target_ref[0, p], source_ref[0, p]
            spread_targets(tgt_ref, tile, tb)
            for k in range(3):
                spread(geo, k, src_ref[member, k])
            spread(geo, 3, src_ref[member, AREA_ROW] * (1.0 / 6.0))

            def block_fn(i, carry):
                rows = pl.ds(pl.multiple_of(i * SUBS, SUBS), SUBS)
                coords = [tb[k, rows, :] for k in range(3)]
                for c in range(lines):
                    cols = slice(c * LANES, (c + 1) * LANES)
                    dist_sq = None
                    for k in range(3):
                        delta = coords[k] - geo[k, :, cols]
                        square = delta * delta
                        dist_sq = square if dist_sq is None else dist_sq + square
                    weight = geo[3, :, cols] * lax.rsqrt(dist_sq + SOFTEN)
                    u = 1.0 / (1.0 + dist_sq)
                    square = u * u
                    cube = square * u
                    near_ref[slot, 0, c, rows, :] = weight * cube
                    near_ref[slot, 1, c, rows, :] = weight * (1.0 + 3.0 * (u + square - cube))
                    near_ref[slot, 2, c, rows, :] = weight * (4.0 + 3.0 * (cube - 2.0 * square))
                return carry

            lax.fori_loop(0, tb.shape[1] // SUBS, block_fn, 0, unroll=tb.shape[1] // SUBS)
        return carry

    lax.fori_loop(0, (count + 1) // 2, turn_fn, 0)


def near_sums(step, near_ref, slot, new_ref, member, lag):
    total = None
    for k in range(step):
        density = new_ref[member, 3 + step - lag - k]
        for c in range(density.shape[0]):
            term = near_ref[slot, k, c] * density[c : c + 1, :]
            total = term if total is None else total + term
    halves = [
        jnp.sum(jnp.transpose(total[b * LANES : (b + 1) * LANES], (1, 0)), axis=0, keepdims=True) for b in range(2)
    ]
    return jnp.concatenate(halves, axis=0)


def thirds(row):
    high = row.astype(jnp.bfloat16)
    rest = row - high.astype(jnp.float32)
    middle = rest.astype(jnp.bfloat16)
    low = (rest - middle.astype(jnp.float32)).astype(jnp.bfloat16)
    return jnp.concatenate([high, middle, low, jnp.zeros((13, row.shape[1]), jnp.bfloat16)], axis=0)


def one_hot_dot(row, chosen, contract):
    parts = lax.dot_general(thirds(row), chosen, (((1,), (contract,)), ((), ())), preferred_element_type=jnp.float32)
    return parts[0:1, :] + (parts[1:2, :] + parts[2:3, :])


def one_hot(index_ref, nodes):
    node = lax.broadcasted_iota(jnp.int32, (nodes, index_ref.shape[1]), 0)
    return jnp.where(node == index_ref[...], 1.0, 0.0).astype(jnp.bfloat16)


def pick_trace(density, send_ref):
    return one_hot_dot(density, one_hot(send_ref, density.shape[1]), 0)


def junction_of(trace, recv_ref, gain_ref, nodes):
    return one_hot_dot(trace * gain_ref[...], one_hot(recv_ref, nodes), 1)


def step_kernel(
    step, order_ref, target_ref, source_ref, lag_ref, place_ref, near_ref, tgt_ref, src_ref, send_ref, own_ref, *refs
):
    new_refs = refs[:step]
    out_ref, new = refs[step : step + 2]
    work = refs[step + 2 :]
    region, group = place_ref[0], place_ref[2]
    out_ref[...] = jnp.zeros_like(out_ref)
    new[...] = jnp.zeros_like(new)
    for j in range(step):
        new[:, 3 + j] = new_refs[j][...]
    trace = pick_trace(own_ref[...], send_ref)
    tiles = tgt_ref.shape[0] * 2
    for other in range(out_ref.shape[0] // tiles):

        @pl.when(other != region)
        def _():
            out_ref[other * tiles + 2 * group] = jnp.concatenate([trace, trace], axis=0)

    def window_of(member, lag):
        return [new[member, step - lag + i] for i in range(4)]

    def add(tile, rows):
        out_ref[region * tiles + tile] += rows

    count = order_ref[target_ref.shape[1] + step - 1]
    kept = jnp.minimum(count, NEAR)

    def turn_fn(turn, carry):
        sums = []
        for side in range(2):
            place = 2 * turn + side
            slot = jnp.minimum(place, kept - 1)
            p = order_ref[slot]
            share = near_sums(step, near_ref, slot, new, source_ref[0, p], lag_ref[0, p])
            sums.append((target_ref[0, p], jnp.where(place < kept, share, 0.0)))
        for tile, share in sums:
            add(tile, share)
        return carry

    lax.fori_loop(0, (kept + 1) // 2, turn_fn, 0)
    lists = (target_ref, source_ref, lag_ref)
    two_at_a_time(
        count - kept, lambda p: order_ref[NEAR + p], lists, tgt_ref, src_ref, (work[:4], work[4:]), 1, window_of, add
    )


def first_trace_kernel(send_ref, hist_ref, trace_ref):
    trace = pick_trace(hist_ref[HIST - 1 : HIST, :], send_ref)
    for r in range(trace_ref.shape[0]):
        trace_ref[r] = trace


def density_kernel(step, place_ref, part_ref, recv_ref, gain_ref, inc_ref, self_ref, *refs):
    nodes = inc_ref.shape[1]
    region, partner, group = place_ref[0], place_ref[1], place_ref[2]
    last = step == STEPS - 1
    if step == 0:
        trace_ref, dens_ref, row_ref, past_ref = refs
        groups = part_ref.shape[0] // 2
        fields = []
        for h in range(2):
            total = part_ref[h]
            for g in range(1, groups):
                total = total + part_ref[2 * g + h]
            fields.append(total)
        past = jnp.concatenate(fields, axis=0)
        past_ref[...] = past
        trace = trace_ref[partner]
        rows = [past[8 * h + b : 8 * h + b + 1, :] for h in range(2) for b in range(2)]
    else:
        past_ref = refs[0]
        groups = part_ref.shape[0] // 8
        first = region * (2 * groups)
        rows = []
        for h in range(2):
            total = past_ref[8 * h + 2 * step : 8 * h + 2 * step + 2, :]
            for g in range(groups):
                total = total + part_ref[first + 2 * g + h]
            rows += [total[0:1, :], total[1:2, :]]
        trace = part_ref[(partner * groups + group) * 2][0:1, :]
    field = jnp.concatenate(rows, axis=1)
    junction = junction_of(trace, recv_ref, gain_ref, nodes)
    density = (inc_ref[step : step + 1, :] - field - junction) / self_ref[...]
    if last:
        row_refs, out_ref = refs[1:-1], refs[-1]
        for n in range(STEPS - 1):
            out_ref[n : n + 1, :] = row_refs[n][...]
        out_ref[STEPS - 1 : STEPS, :] = density
    else:
        if step > 0:
            dens_ref, row_ref = refs[1:]
        row_ref[...] = density
        for r in range(nodes // LANES):
            part = density[:, r * LANES : (r + 1) * LANES]
            dens_ref[:, r, :] = jnp.broadcast_to(part, (dens_ref.shape[0], LANES))


def body(
    history,
    incident,
    positions,
    area,
    self_weight,
    pair_target,
    pair_source,
    pair_lag,
    pair_count,
    junc_send,
    junc_recv,
    junc_gain,
    adjacency,
):
    nodes = history.shape[1]
    half = nodes // 2
    jrows = junc_send.shape[1]
    groups, regions, loops = (lax.axis_size(name) for name in ("group", "region", "loop"))
    tiles = 2 * groups
    f32 = jnp.float32
    shape = jax.ShapeDtypeStruct
    region = lax.axis_index("region")
    place = jnp.stack([region, (region + adjacency[0]) % regions, lax.axis_index("group")]).astype(jnp.int32)
    self_row = self_weight.reshape(1, nodes)
    lists = (pair_target, pair_source, pair_lag)
    line_rows = nodes // LANES

    packed = jnp.concatenate([positions, area[None], history[FIRST_STORED:]], axis=0)
    packed = packed.reshape(packed.shape[0], line_rows, LANES)
    packed = jnp.broadcast_to(packed, (loops,) + packed.shape)
    sources = lax.all_to_all(packed, "loop", 0, 0, tiled=True)
    targets = lax.all_to_all(jnp.broadcast_to(positions, (groups, 3, nodes)), "group", 0, 0, tiled=True)
    order = pl.pallas_call(
        order_kernel,
        out_shape=shape((pair_lag.shape[1] + STEPS,), jnp.int32),
        in_specs=[SMEM] * 2,
        out_specs=SMEM,
        compiler_params=SMALL_GRANT,
    )(pair_count, pair_lag)
    trace = pl.pallas_call(
        first_trace_kernel,
        out_shape=shape((regions, 1, jrows), f32),
        in_specs=[VMEM] * 2,
        out_specs=VMEM,
        compiler_params=SMALL_GRANT,
    )(junc_send, history)
    traces = lax.all_to_all(trace, "region", 0, 0, tiled=True)

    def work(steps):
        return [
            pltpu.VMEM((3, half, LANES), f32),
            pltpu.VMEM((3, SUBS, nodes), f32),
            pltpu.VMEM((steps * COEFS, SUBS, nodes), f32),
            pltpu.VMEM((steps, half, LANES), f32),
        ]

    partial_fields = pl.pallas_call(
        history_kernel,
        out_shape=shape((tiles, 2 * STEPS, LANES), f32),
        in_specs=[SMEM] * 4 + [VMEM] * 2,
        out_specs=VMEM,
        scratch_shapes=work(STEPS) * 2,
        compiler_params=PAIR_GRANT,
    )(order, *lists, targets, sources)
    order, place, partial_fields, traces = lax.optimization_barrier((order, place, partial_fields, traces))
    near = pl.pallas_call(
        near_kernel,
        out_shape=shape((NEAR, NEAR_COEFS, line_rows, half, LANES), f32),
        in_specs=[SMEM] * 3 + [VMEM] * 2,
        out_specs=VMEM,
        scratch_shapes=[pltpu.VMEM((3, half, LANES), f32), pltpu.VMEM((4, SUBS, nodes), f32)] * 2,
        compiler_params=NEAR_GRANT,
    )(order, pair_target, pair_source, targets, sources)
    near, partial_fields = lax.optimization_barrier((near, partial_fields))
    parts = lax.all_to_all(partial_fields, "group", 0, 0, tiled=True)

    dens_shape, row_shape = shape((loops, line_rows, LANES), f32), shape((1, nodes), f32)
    rows, gathered = [], []
    past = None
    for step in range(STEPS):
        if step > 0:
            partial_fields = pl.pallas_call(
                functools.partial(step_kernel, step),
                out_shape=shape((regions * tiles, 2, LANES), f32),
                in_specs=[SMEM] * 5 + [VMEM] * (5 + step),
                out_specs=VMEM,
                scratch_shapes=[pltpu.VMEM((loops, SUBS, line_rows, LANES), f32)] + work(1) * 2,
                compiler_params=NEAR_GRANT,
            )(order, *lists, place, near, targets, sources, junc_send, rows[-1], *gathered)
            parts = lax.all_to_all(partial_fields, ("region", "group"), 0, 0, tiled=True)
        operands = [place, parts, junc_recv, junc_gain, incident, self_row]
        if step == 0:
            operands += [traces]
            out_shape = [dens_shape, row_shape, shape((2 * 2 * STEPS, LANES), f32)]
        elif step < STEPS - 1:
            operands += [past]
            out_shape = [dens_shape, row_shape]
        else:
            operands += [past] + rows
            out_shape = [shape((STEPS, nodes), f32)]
        results = pl.pallas_call(
            functools.partial(density_kernel, step),
            out_shape=out_shape,
            in_specs=[SMEM] + [VMEM] * (len(operands) - 1),
            out_specs=[VMEM] * len(out_shape),
            compiler_params=SMALL_GRANT,
        )(*operands)
        if step == 0:
            past = results[2]
        if step < STEPS - 1:
            rows.append(results[1])
            gathered.append(lax.all_to_all(results[0], "loop", 0, 0, tiled=True))
    return results[0]


def solution(mesh):
    blocks = ("region", "group", "loop")
    in_specs = (
        P(None, blocks),
        P(None, blocks),
        P(None, blocks),
        P(blocks),
        P(blocks),
        P(blocks, None),
        P(blocks, None),
        P(blocks, None),
        P(blocks),
        P(blocks, None),
        P(blocks, None),
        P(blocks, None),
        P(blocks),
    )
    return jax.shard_map(body, mesh=mesh, in_specs=in_specs, out_specs=P(None, blocks), check_vma=False)
```

```python
import functools

import jax
import jax.numpy as jnp
from jax import lax
from jax.experimental import pallas as pl
from jax.experimental.pallas import tpu as pltpu
from jax.sharding import PartitionSpec as P


HIST = 16
STEPS = 4
LANES = 128
SUBS = 8
SOFTEN = 0.25
AREA_ROW = 3
STORED_ROW = 4
FIRST_STORED = 1
COEFS = 4
NEAR = 12
NEAR_COEFS = STEPS - 1


PAIR_GRANT = pltpu.CompilerParams(vmem_limit_bytes=12 * 2**20)
NEAR_GRANT = pltpu.CompilerParams(vmem_limit_bytes=12 * 2**20)
SMALL_GRANT = pltpu.CompilerParams(vmem_limit_bytes=4 * 2**20)
VMEM = pl.BlockSpec(memory_space=pltpu.VMEM)
SMEM = pl.BlockSpec(memory_space=pltpu.SMEM)


def spline_coefs(rows, scale):
    d, c, b, a = rows
    return (
        (b + 4.0 * c + d) * scale,
        3.0 * (b - d) * scale,
        3.0 * (b - 2.0 * c + d) * scale,
        (a - d + 3.0 * (c - b)) * scale,
    )


def spread_targets(tgt_ref, tile, tb_ref):
    group, start = tile // 2, (tile % 2) * (2 * LANES)
    for k in range(3):
        for b in range(2):
            row = tgt_ref[group, k : k + 1, pl.ds(pl.multiple_of(start + b * LANES, LANES), LANES)]
            tb_ref[k, b * LANES : (b + 1) * LANES, :] = jnp.transpose(jnp.broadcast_to(row, (LANES, LANES)), (1, 0))


def pair_sums(steps, nodes, tb_ref, geo_ref, coef_ref, acc_ref):
    def block_fn(i, carry):
        rows = pl.ds(pl.multiple_of(i * SUBS, SUBS), SUBS)
        coords = [tb_ref[k, rows, :] for k in range(3)]
        sums = [None] * steps
        for c in range(nodes // LANES):
            cols = slice(c * LANES, (c + 1) * LANES)
            dist_sq = None
            for k in range(3):
                delta = coords[k] - geo_ref[k, :, cols]
                square = delta * delta
                dist_sq = square if dist_sq is None else dist_sq + square
            weight = lax.rsqrt(dist_sq + SOFTEN)
            u = 1.0 / (1.0 + dist_sq)
            for n in range(steps):
                mix = coef_ref[n * COEFS + 3, :, cols]
                for power in (2, 1, 0):
                    mix = mix * u + coef_ref[n * COEFS + power, :, cols]
                term = weight * mix
                sums[n] = term if sums[n] is None else sums[n] + term
        for n in range(steps):
            acc_ref[n, rows, :] = sums[n]
        return carry

    lax.fori_loop(0, acc_ref.shape[1] // SUBS, block_fn, 0, unroll=acc_ref.shape[1] // SUBS)


def lane_totals(acc_ref, n):
    return [
        jnp.sum(jnp.transpose(acc_ref[n, b * LANES : (b + 1) * LANES, :], (1, 0)), axis=0, keepdims=True)
        for b in range(2)
    ]


def spread(ref, index, lines):
    for c in range(lines.shape[0]):
        ref[index, :, c * LANES : (c + 1) * LANES] = jnp.broadcast_to(lines[c : c + 1, :], (SUBS, LANES))


class Span:
    def __init__(self, ref, start):
        self.ref, self.start = ref, start

    def __getitem__(self, index):
        return self.ref[self.start + index]


class Plan:
    def __init__(self, ref):
        pairs = (ref.shape[0] - STEPS - 3) // 4
        self.near = Span(ref, 0)
        self.upto = Span(ref, pairs - 1)
        self.count = Span(ref, pairs + STEPS - 1)
        self.target, self.source, self.lag = (Span(ref, pairs * i + STEPS) for i in (1, 2, 3))
        self.place = Span(ref, 4 * pairs + STEPS)


def write_plan(count_ref, target_ref, source_ref, lag_ref, adjacency_ref, plan_ref):
    pairs, count = lag_ref.shape[1], count_ref[0]
    lags = [jnp.where(p < count, lag_ref[0, p], 0) for p in range(pairs)]
    filled = jnp.int32(0)
    ends = []
    for lag in range(1, STEPS):
        for p in range(pairs):
            plan_ref[filled] = p
            filled = filled + (lags[p] == lag).astype(jnp.int32)
        ends.append(filled)
    for place, end in enumerate(ends + [count]):
        plan_ref[pairs + place] = end
    for i, ref in enumerate((target_ref, source_ref, lag_ref)):
        for p in range(pairs):
            plan_ref[pairs * (i + 1) + STEPS + p] = ref[0, p]
    region, regions = lax.axis_index("region"), lax.axis_size("region")
    own = (region, lax.rem(region + adjacency_ref[0], regions), lax.axis_index("group"))
    for i, value in enumerate(own):
        plan_ref[4 * pairs + STEPS + i] = value


def two_at_a_time(count, pick, plan, tgt_ref, src_ref, works, steps, window_of, add):
    nodes = src_ref.shape[2] * LANES

    def turn_fn(turn, carry):
        tiles = []
        for side, (tb, geo, coef, acc) in enumerate(works):
            place = 2 * turn + side
            p = pick(jnp.minimum(place, count - 1))
            tile, member, lag = plan.target[p], plan.source[p], plan.lag[p]
            factor = jnp.where(place < count, 1.0 / 6.0, 0.0)
            spread_targets(tgt_ref, tile, tb)
            for k in range(3):
                spread(geo, k, src_ref[member, k])
            scale = src_ref[member, AREA_ROW] * factor
            window = window_of(member, lag)
            for n in range(steps):
                for power, value in enumerate(spline_coefs(window[n : n + 4], scale)):
                    spread(coef, n * COEFS + power, value)
            pair_sums(steps, nodes, tb, geo, coef, acc)
            tiles.append(tile)
        for tile, (_, _, _, acc) in zip(tiles, works):
            add(tile, jnp.concatenate([row for n in range(steps) for row in lane_totals(acc, n)], axis=0))
        return carry

    lax.fori_loop(0, (count + 1) // 2, turn_fn, 0)


def history_kernel(plan_ref, tgt_ref, src_ref, out_ref, *work):
    out_ref[...] = jnp.zeros_like(out_ref)

    def window_of(member, lag):
        first, end = STORED_ROW - FIRST_STORED + HIST - 3 - lag, src_ref.shape[1]
        rows = [src_ref[member, first + i] for i in range(4)]
        for i in range(4, STEPS + 3):
            row = src_ref[member, jnp.minimum(first + i, end - 1)]
            rows.append(jnp.where(first + i < end, row, 0.0))
        return rows

    def add(tile, rows):
        out_ref[tile] += rows

    plan = Plan(plan_ref)
    two_at_a_time(plan.count[0], lambda p: p, plan, tgt_ref, src_ref, (work[:4], work[4:]), STEPS, window_of, add)


def near_kernel(plan_ref, tgt_ref, src_ref, near_ref, *work):
    lines = src_ref.shape[2]
    plan = Plan(plan_ref)
    count = jnp.minimum(plan.upto[STEPS - 1], NEAR)
    spaces = (work[:2], work[2:])

    def turn_fn(turn, carry):
        for side, (tb, geo) in enumerate(spaces):
            slot = jnp.minimum(2 * turn + side, count - 1)
            p = plan.near[slot]
            tile, member = plan.target[p], plan.source[p]
            spread_targets(tgt_ref, tile, tb)
            for k in range(3):
                spread(geo, k, src_ref[member, k])
            spread(geo, 3, src_ref[member, AREA_ROW] * (1.0 / 6.0))

            def block_fn(i, carry):
                rows = pl.ds(pl.multiple_of(i * SUBS, SUBS), SUBS)
                coords = [tb[k, rows, :] for k in range(3)]
                for c in range(lines):
                    cols = slice(c * LANES, (c + 1) * LANES)
                    dist_sq = None
                    for k in range(3):
                        delta = coords[k] - geo[k, :, cols]
                        square = delta * delta
                        dist_sq = square if dist_sq is None else dist_sq + square
                    weight = geo[3, :, cols] * lax.rsqrt(dist_sq + SOFTEN)
                    u = 1.0 / (1.0 + dist_sq)
                    square = u * u
                    cube = square * u
                    near_ref[slot, 0, c, rows, :] = weight * cube
                    near_ref[slot, 1, c, rows, :] = weight * (1.0 + 3.0 * (u + square - cube))
                    near_ref[slot, 2, c, rows, :] = weight * (4.0 + 3.0 * (cube - 2.0 * square))
                return carry

            lax.fori_loop(0, tb.shape[1] // SUBS, block_fn, 0, unroll=tb.shape[1] // SUBS)
        return carry

    lax.fori_loop(0, (count + 1) // 2, turn_fn, 0)


def near_sums(step, near_ref, slot, new_ref, member, lag):
    total = None
    for k in range(step):
        density = new_ref[member, 3 + step - lag - k]
        for c in range(density.shape[0]):
            term = near_ref[slot, k, c] * density[c : c + 1, :]
            total = term if total is None else total + term
    halves = [
        jnp.sum(jnp.transpose(total[b * LANES : (b + 1) * LANES], (1, 0)), axis=0, keepdims=True) for b in range(2)
    ]
    return jnp.concatenate(halves, axis=0)


def thirds(row):
    high = row.astype(jnp.bfloat16)
    rest = row - high.astype(jnp.float32)
    middle = rest.astype(jnp.bfloat16)
    low = (rest - middle.astype(jnp.float32)).astype(jnp.bfloat16)
    return jnp.concatenate([high, middle, low, jnp.zeros((13, row.shape[1]), jnp.bfloat16)], axis=0)


def one_hot_dot(row, chosen, contract):
    parts = lax.dot_general(thirds(row), chosen, (((1,), (contract,)), ((), ())), preferred_element_type=jnp.float32)
    return parts[0:1, :] + (parts[1:2, :] + parts[2:3, :])


def one_hot(index_ref, nodes):
    node = lax.broadcasted_iota(jnp.int32, (nodes, index_ref.shape[1]), 0)
    return jnp.where(node == index_ref[...], 1.0, 0.0).astype(jnp.bfloat16)


def pick_trace(density, send_ref):
    return one_hot_dot(density, one_hot(send_ref, density.shape[1]), 0)


def junction_of(trace, recv_ref, gain_ref, nodes):
    return one_hot_dot(trace * gain_ref[...], one_hot(recv_ref, nodes), 1)


def step_kernel(
    step, plan_ref, near_ref, tgt_ref, src_ref, send_ref, own_ref, *refs
):
    new_refs = refs[:step]
    out_ref, new = refs[step : step + 2]
    work = refs[step + 2 :]
    plan = Plan(plan_ref)
    region, group = plan.place[0], plan.place[2]
    out_ref[...] = jnp.zeros_like(out_ref)
    new[...] = jnp.zeros_like(new)
    for j in range(step):
        new[:, 3 + j] = new_refs[j][...]
    trace = pick_trace(own_ref[...], send_ref)
    tiles = tgt_ref.shape[0] * 2
    for other in range(out_ref.shape[0] // tiles):

        @pl.when(other != region)
        def _():
            out_ref[other * tiles + 2 * group] = jnp.concatenate([trace, trace], axis=0)

    def window_of(member, lag):
        return [new[member, step - lag + i] for i in range(4)]

    def add(tile, rows):
        out_ref[region * tiles + tile] += rows

    count = plan.upto[step]
    kept = jnp.minimum(count, NEAR)

    def turn_fn(turn, carry):
        sums = []
        for side in range(2):
            place = 2 * turn + side
            slot = jnp.minimum(place, kept - 1)
            p = plan.near[slot]
            share = near_sums(step, near_ref, slot, new, plan.source[p], plan.lag[p])
            sums.append((plan.target[p], jnp.where(place < kept, share, 0.0)))
        for tile, share in sums:
            add(tile, share)
        return carry

    lax.fori_loop(0, (kept + 1) // 2, turn_fn, 0)
    two_at_a_time(
        count - kept, lambda p: plan.near[NEAR + p], plan, tgt_ref, src_ref, (work[:4], work[4:]), 1, window_of, add
    )


def prepare_kernel(*refs):
    write_plan(*refs[:5], refs[9])
    positions, area, history, send = refs[5:9]
    packed_ref, trace_ref = refs[10:]
    rows = [positions[k : k + 1, :] for k in range(3)] + [area[...]]
    rows += [history[k : k + 1, :] for k in range(FIRST_STORED, HIST)]
    lines = packed_ref.shape[2]
    for i, row in enumerate(rows):
        block = jnp.concatenate([row[:, c * LANES : (c + 1) * LANES] for c in range(lines)], axis=0)
        for member in range(packed_ref.shape[0]):
            packed_ref[member, i] = block
    trace = pick_trace(history[HIST - 1 : HIST, :], send)
    for r in range(trace_ref.shape[0]):
        trace_ref[r] = trace


def density_kernel(step, plan_ref, part_ref, recv_ref, gain_ref, inc_ref, self_ref, *refs):
    nodes = inc_ref.shape[1]
    place = Plan(plan_ref).place
    region, partner, group = place[0], place[1], place[2]
    last = step == STEPS - 1
    if step == 0:
        trace_ref, dens_ref, row_ref, past_ref = refs
        groups = part_ref.shape[0] // 2
        fields = []
        for h in range(2):
            total = part_ref[h]
            for g in range(1, groups):
                total = total + part_ref[2 * g + h]
            fields.append(total)
        past = jnp.concatenate(fields, axis=0)
        past_ref[...] = past
        trace = trace_ref[partner]
        rows = [past[8 * h + b : 8 * h + b + 1, :] for h in range(2) for b in range(2)]
    else:
        past_ref = refs[0]
        groups = part_ref.shape[0] // 8
        first = region * (2 * groups)
        rows = []
        for h in range(2):
            total = past_ref[8 * h + 2 * step : 8 * h + 2 * step + 2, :]
            for g in range(groups):
                total = total + part_ref[first + 2 * g + h]
            rows += [total[0:1, :], total[1:2, :]]
        trace = part_ref[(partner * groups + group) * 2][0:1, :]
    field = jnp.concatenate(rows, axis=1)
    junction = junction_of(trace, recv_ref, gain_ref, nodes)
    density = (inc_ref[step : step + 1, :] - field - junction) / self_ref[...]
    if last:
        row_refs, out_ref = refs[1:-1], refs[-1]
        for n in range(STEPS - 1):
            out_ref[n : n + 1, :] = row_refs[n][...]
        out_ref[STEPS - 1 : STEPS, :] = density
    else:
        if step > 0:
            dens_ref, row_ref = refs[1:]
        row_ref[...] = density
        for r in range(nodes // LANES):
            part = density[:, r * LANES : (r + 1) * LANES]
            dens_ref[:, r, :] = jnp.broadcast_to(part, (dens_ref.shape[0], LANES))


def body(
    history,
    incident,
    positions,
    area,
    self_weight,
    pair_target,
    pair_source,
    pair_lag,
    pair_count,
    junc_send,
    junc_recv,
    junc_gain,
    adjacency,
):
    nodes = history.shape[1]
    half = nodes // 2
    jrows = junc_send.shape[1]
    groups, regions, loops = (lax.axis_size(name) for name in ("group", "region", "loop"))
    tiles = 2 * groups
    f32 = jnp.float32
    shape = jax.ShapeDtypeStruct
    self_row = self_weight.reshape(1, nodes)
    line_rows = nodes // LANES

    given = (pair_count, pair_target, pair_source, pair_lag, adjacency)
    arrays = (positions, area.reshape(1, nodes), history, junc_send)
    plan, packed, trace = pl.pallas_call(
        prepare_kernel,
        out_shape=(
            shape((4 * pair_lag.shape[1] + STEPS + 3,), jnp.int32),
            shape((loops, STORED_ROW + HIST - FIRST_STORED, line_rows, LANES), f32),
            shape((regions, 1, jrows), f32),
        ),
        in_specs=[SMEM] * 5 + [VMEM] * 4,
        out_specs=(SMEM, VMEM, VMEM),
    )(*given, *arrays)
    sources = lax.all_to_all(packed, "loop", 0, 0, tiled=True)
    targets = lax.all_to_all(jnp.broadcast_to(positions, (groups, 3, nodes)), "group", 0, 0, tiled=True)
    traces = lax.all_to_all(trace, "region", 0, 0, tiled=True)

    def work(steps):
        return [
            pltpu.VMEM((3, half, LANES), f32),
            pltpu.VMEM((3, SUBS, nodes), f32),
            pltpu.VMEM((steps * COEFS, SUBS, nodes), f32),
            pltpu.VMEM((steps, half, LANES), f32),
        ]

    partial_fields = pl.pallas_call(
        history_kernel,
        out_shape=shape((tiles, 2 * STEPS, LANES), f32),
        in_specs=[SMEM] + [VMEM] * 2,
        out_specs=VMEM,
        scratch_shapes=work(STEPS) * 2,
        compiler_params=PAIR_GRANT,
    )(plan, targets, sources)
    plan, partial_fields, traces = lax.optimization_barrier((plan, partial_fields, traces))
    near = pl.pallas_call(
        near_kernel,
        out_shape=shape((NEAR, NEAR_COEFS, line_rows, half, LANES), f32),
        in_specs=[SMEM] + [VMEM] * 2,
        out_specs=VMEM,
        scratch_shapes=[pltpu.VMEM((3, half, LANES), f32), pltpu.VMEM((4, SUBS, nodes), f32)] * 2,
        compiler_params=NEAR_GRANT,
    )(plan, targets, sources)
    near, partial_fields = lax.optimization_barrier((near, partial_fields))
    parts = lax.all_to_all(partial_fields, "group", 0, 0, tiled=True)

    dens_shape, row_shape = shape((loops, line_rows, LANES), f32), shape((1, nodes), f32)
    rows, gathered = [], []
    past = None
    for step in range(STEPS):
        if step > 0:
            partial_fields = pl.pallas_call(
                functools.partial(step_kernel, step),
                out_shape=shape((regions * tiles, 2, LANES), f32),
                in_specs=[SMEM] + [VMEM] * (5 + step),
                out_specs=VMEM,
                scratch_shapes=[pltpu.VMEM((loops, SUBS, line_rows, LANES), f32)] + work(1) * 2,
                compiler_params=NEAR_GRANT,
            )(plan, near, targets, sources, junc_send, rows[-1], *gathered)
            parts = lax.all_to_all(partial_fields, ("region", "group"), 0, 0, tiled=True)
        operands = [plan, parts, junc_recv, junc_gain, incident, self_row]
        if step == 0:
            operands += [traces]
            out_shape = [dens_shape, row_shape, shape((2 * 2 * STEPS, LANES), f32)]
        elif step < STEPS - 1:
            operands += [past]
            out_shape = [dens_shape, row_shape]
        else:
            operands += [past] + rows
            out_shape = [shape((STEPS, nodes), f32)]
        results = pl.pallas_call(
            functools.partial(density_kernel, step),
            out_shape=out_shape,
            in_specs=[SMEM] + [VMEM] * (len(operands) - 1),
            out_specs=[VMEM] * len(out_shape),
            compiler_params=SMALL_GRANT,
        )(*operands)
        if step == 0:
            past = results[2]
        if step < STEPS - 1:
            rows.append(results[1])
            gathered.append(lax.all_to_all(results[0], "loop", 0, 0, tiled=True))
    return results[0]


def solution(mesh):
    blocks = ("region", "group", "loop")
    in_specs = (
        P(None, blocks),
        P(None, blocks),
        P(None, blocks),
        P(blocks),
        P(blocks),
        P(blocks, None),
        P(blocks, None),
        P(blocks, None),
        P(blocks),
        P(blocks, None),
        P(blocks, None),
        P(blocks, None),
        P(blocks),
    )
    return jax.shard_map(body, mesh=mesh, in_specs=in_specs, out_specs=P(None, blocks), check_vma=False)
```

```python
import functools

import jax
import jax.numpy as jnp
from jax import lax
from jax.experimental import pallas as pl
from jax.experimental.pallas import tpu as pltpu
from jax.sharding import PartitionSpec as P


HIST = 16
STEPS = 4
LANES = 128
SUBS = 8
SOFTEN = 0.25
AREA_ROW = 3
STORED_ROW = 4
FIRST_STORED = 1
COEFS = 4
NEAR = 12
NEAR_COEFS = STEPS - 1


PAIR_GRANT = pltpu.CompilerParams(vmem_limit_bytes=12 * 2**20)
NEAR_GRANT = pltpu.CompilerParams(vmem_limit_bytes=12 * 2**20)
SMALL_GRANT = pltpu.CompilerParams(vmem_limit_bytes=4 * 2**20)
VMEM = pl.BlockSpec(memory_space=pltpu.VMEM)
SMEM = pl.BlockSpec(memory_space=pltpu.SMEM)


def spline_coefs(rows, scale):
    d, c, b, a = rows
    return (
        (b + 4.0 * c + d) * scale,
        3.0 * (b - d) * scale,
        3.0 * (b - 2.0 * c + d) * scale,
        (a - d + 3.0 * (c - b)) * scale,
    )


def spread_targets(tgt_ref, tile, tb_ref):
    group, start = tile // 2, (tile % 2) * (2 * LANES)
    for k in range(3):
        for b in range(2):
            row = tgt_ref[group, k : k + 1, pl.ds(pl.multiple_of(start + b * LANES, LANES), LANES)]
            tb_ref[k, b * LANES : (b + 1) * LANES, :] = jnp.transpose(jnp.broadcast_to(row, (LANES, LANES)), (1, 0))


def pair_sums(steps, nodes, tb_ref, geo_ref, coef_ref, acc_ref):
    def block_fn(i, carry):
        rows = pl.ds(pl.multiple_of(i * SUBS, SUBS), SUBS)
        coords = [tb_ref[k, rows, :] for k in range(3)]
        sums = [None] * steps
        for c in range(nodes // LANES):
            cols = slice(c * LANES, (c + 1) * LANES)
            dist_sq = None
            for k in range(3):
                delta = coords[k] - geo_ref[k, :, cols]
                square = delta * delta
                dist_sq = square if dist_sq is None else dist_sq + square
            weight = lax.rsqrt(dist_sq + SOFTEN)
            u = 1.0 / (1.0 + dist_sq)
            for n in range(steps):
                mix = coef_ref[n * COEFS + 3, :, cols]
                for power in (2, 1, 0):
                    mix = mix * u + coef_ref[n * COEFS + power, :, cols]
                term = weight * mix
                sums[n] = term if sums[n] is None else sums[n] + term
        for n in range(steps):
            acc_ref[n, rows, :] = sums[n]
        return carry

    lax.fori_loop(0, acc_ref.shape[1] // SUBS, block_fn, 0, unroll=acc_ref.shape[1] // SUBS)


def lane_totals(acc_ref, n):
    return [
        jnp.sum(jnp.transpose(acc_ref[n, b * LANES : (b + 1) * LANES, :], (1, 0)), axis=0, keepdims=True)
        for b in range(2)
    ]


def spread(ref, index, lines):
    for c in range(lines.shape[0]):
        ref[index, :, c * LANES : (c + 1) * LANES] = jnp.broadcast_to(lines[c : c + 1, :], (SUBS, LANES))


class Span:
    def __init__(self, ref, start):
        self.ref, self.start = ref, start

    def __getitem__(self, index):
        return self.ref[self.start + index]


class Plan:
    def __init__(self, ref):
        pairs = (ref.shape[0] - STEPS - 3) // 4
        self.near = Span(ref, 0)
        self.upto = Span(ref, pairs - 1)
        self.count = Span(ref, pairs + STEPS - 1)
        self.target, self.source, self.lag = (Span(ref, pairs * i + STEPS) for i in (1, 2, 3))
        self.place = Span(ref, 4 * pairs + STEPS)


def write_plan(count_ref, target_ref, source_ref, lag_ref, adjacency_ref, plan_ref):
    pairs, count = lag_ref.shape[1], count_ref[0]
    lags = [jnp.where(p < count, lag_ref[0, p], 0) for p in range(pairs)]
    filled = jnp.int32(0)
    ends = []
    for lag in range(1, STEPS):
        for p in range(pairs):
            plan_ref[filled] = p
            filled = filled + (lags[p] == lag).astype(jnp.int32)
        ends.append(filled)
    for place, end in enumerate(ends + [count]):
        plan_ref[pairs + place] = end
    for i, ref in enumerate((target_ref, source_ref, lag_ref)):
        for p in range(pairs):
            plan_ref[pairs * (i + 1) + STEPS + p] = ref[0, p]
    region, regions = lax.axis_index("region"), lax.axis_size("region")
    own = (region, lax.rem(region + adjacency_ref[0], regions), lax.axis_index("group"))
    for i, value in enumerate(own):
        plan_ref[4 * pairs + STEPS + i] = value


def two_at_a_time(count, pick, plan, tgt_ref, src_ref, works, steps, window_of, add):
    nodes = src_ref.shape[2] * LANES

    def turn_fn(turn, carry):
        tiles = []
        for side, (tb, geo, coef, acc) in enumerate(works):
            place = 2 * turn + side
            p = pick(jnp.minimum(place, count - 1))
            tile, member, lag = plan.target[p], plan.source[p], plan.lag[p]
            factor = jnp.where(place < count, 1.0 / 6.0, 0.0)
            spread_targets(tgt_ref, tile, tb)
            for k in range(3):
                spread(geo, k, src_ref[member, k])
            scale = src_ref[member, AREA_ROW] * factor
            window = window_of(member, lag)
            for n in range(steps):
                for power, value in enumerate(spline_coefs(window[n : n + 4], scale)):
                    spread(coef, n * COEFS + power, value)
            pair_sums(steps, nodes, tb, geo, coef, acc)
            tiles.append(tile)
        for tile, (_, _, _, acc) in zip(tiles, works):
            add(tile, jnp.concatenate([row for n in range(steps) for row in lane_totals(acc, n)], axis=0))
        return carry

    lax.fori_loop(0, (count + 1) // 2, turn_fn, 0)


def history_kernel(plan_ref, tgt_ref, src_ref, out_ref, *work):
    out_ref[...] = jnp.zeros_like(out_ref)

    def window_of(member, lag):
        first, end = STORED_ROW - FIRST_STORED + HIST - 3 - lag, src_ref.shape[1]
        rows = [src_ref[member, first + i] for i in range(4)]
        for i in range(4, STEPS + 3):
            row = src_ref[member, jnp.minimum(first + i, end - 1)]
            rows.append(jnp.where(first + i < end, row, 0.0))
        return rows

    def add(tile, rows):
        out_ref[tile] += rows

    plan = Plan(plan_ref)
    two_at_a_time(plan.count[0], lambda p: p, plan, tgt_ref, src_ref, (work[:4], work[4:]), STEPS, window_of, add)


def near_kernel(plan_ref, tgt_ref, src_ref, near_ref, *work):
    lines = src_ref.shape[2]
    plan = Plan(plan_ref)
    count = jnp.minimum(plan.upto[STEPS - 1], NEAR)
    spaces = (work[:2], work[2:])

    def run(turn, kinds):
        for side, (tb, geo) in enumerate(spaces):
            slot = jnp.minimum(2 * turn + side, count - 1)
            p = plan.near[slot]
            tile, member = plan.target[p], plan.source[p]
            spread_targets(tgt_ref, tile, tb)
            for k in range(3):
                spread(geo, k, src_ref[member, k])
            spread(geo, 3, src_ref[member, AREA_ROW] * (1.0 / 6.0))

            def block_fn(i, carry):
                rows = pl.ds(pl.multiple_of(i * SUBS, SUBS), SUBS)
                coords = [tb[k, rows, :] for k in range(3)]
                for c in range(lines):
                    cols = slice(c * LANES, (c + 1) * LANES)
                    dist_sq = None
                    for k in range(3):
                        delta = coords[k] - geo[k, :, cols]
                        square = delta * delta
                        dist_sq = square if dist_sq is None else dist_sq + square
                    weight = geo[3, :, cols] * lax.rsqrt(dist_sq + SOFTEN)
                    u = 1.0 / (1.0 + dist_sq)
                    square = u * u
                    cube = square * u
                    values = [
                        weight * cube,
                        weight * (1.0 + 3.0 * (u + square - cube)) if kinds > 1 else None,
                        weight * (4.0 + 3.0 * (cube - 2.0 * square)) if kinds > 2 else None,
                    ]
                    for kind, value in enumerate(values):
                        near_ref[slot, kind, c, rows, :] = jnp.zeros_like(cube) if value is None else value
                return carry

            lax.fori_loop(0, tb.shape[1] // SUBS, block_fn, 0, unroll=tb.shape[1] // SUBS)

    def turn_fn(turn, carry):
        lead = plan.lag[plan.near[2 * turn]]
        for kinds in range(1, STEPS):

            @pl.when(lead == STEPS - kinds)
            def _(kinds=kinds):
                run(turn, kinds)

        return carry

    lax.fori_loop(0, (count + 1) // 2, turn_fn, 0)


def near_sums(step, near_ref, slot, new_ref, member, lag):
    total = None
    for k in range(step):
        density = new_ref[member, 3 + step - lag - k]
        for c in range(density.shape[0]):
            term = near_ref[slot, k, c] * density[c : c + 1, :]
            total = term if total is None else total + term
    halves = [
        jnp.sum(jnp.transpose(total[b * LANES : (b + 1) * LANES], (1, 0)), axis=0, keepdims=True) for b in range(2)
    ]
    return jnp.concatenate(halves, axis=0)


def thirds(row):
    high = row.astype(jnp.bfloat16)
    rest = row - high.astype(jnp.float32)
    middle = rest.astype(jnp.bfloat16)
    low = (rest - middle.astype(jnp.float32)).astype(jnp.bfloat16)
    return jnp.concatenate([high, middle, low, jnp.zeros((13, row.shape[1]), jnp.bfloat16)], axis=0)


def one_hot_dot(row, chosen, contract):
    parts = lax.dot_general(thirds(row), chosen, (((1,), (contract,)), ((), ())), preferred_element_type=jnp.float32)
    return parts[0:1, :] + (parts[1:2, :] + parts[2:3, :])


def one_hot(index_ref, nodes):
    node = lax.broadcasted_iota(jnp.int32, (nodes, index_ref.shape[1]), 0)
    return jnp.where(node == index_ref[...], 1.0, 0.0).astype(jnp.bfloat16)


def pick_trace(density, send_ref):
    return one_hot_dot(density, one_hot(send_ref, density.shape[1]), 0)


def junction_of(trace, recv_ref, gain_ref, nodes):
    return one_hot_dot(trace * gain_ref[...], one_hot(recv_ref, nodes), 1)


def step_kernel(
    step, plan_ref, near_ref, tgt_ref, src_ref, send_ref, own_ref, *refs
):
    new_refs = refs[:step]
    out_ref, new = refs[step : step + 2]
    work = refs[step + 2 :]
    plan = Plan(plan_ref)
    region, group = plan.place[0], plan.place[2]
    out_ref[...] = jnp.zeros_like(out_ref)
    new[...] = jnp.zeros_like(new)
    for j in range(step):
        new[:, 3 + j] = new_refs[j][...]
    trace = pick_trace(own_ref[...], send_ref)
    tiles = tgt_ref.shape[0] * 2
    for other in range(out_ref.shape[0] // tiles):

        @pl.when(other != region)
        def _():
            out_ref[other * tiles + 2 * group] = jnp.concatenate([trace, trace], axis=0)

    def window_of(member, lag):
        return [new[member, step - lag + i] for i in range(4)]

    def add(tile, rows):
        out_ref[region * tiles + tile] += rows

    count = plan.upto[step]
    kept = jnp.minimum(count, NEAR)

    def turn_fn(turn, carry):
        sums = []
        for side in range(2):
            place = 2 * turn + side
            slot = jnp.minimum(place, kept - 1)
            p = plan.near[slot]
            share = near_sums(step, near_ref, slot, new, plan.source[p], plan.lag[p])
            sums.append((plan.target[p], jnp.where(place < kept, share, 0.0)))
        for tile, share in sums:
            add(tile, share)
        return carry

    lax.fori_loop(0, (kept + 1) // 2, turn_fn, 0)
    two_at_a_time(
        count - kept, lambda p: plan.near[NEAR + p], plan, tgt_ref, src_ref, (work[:4], work[4:]), 1, window_of, add
    )


def prepare_kernel(*refs):
    write_plan(*refs[:5], refs[9])
    positions, area, history, send = refs[5:9]
    packed_ref, trace_ref = refs[10:]
    rows = [positions[k : k + 1, :] for k in range(3)] + [area[...]]
    rows += [history[k : k + 1, :] for k in range(FIRST_STORED, HIST)]
    lines = packed_ref.shape[2]
    for i, row in enumerate(rows):
        block = jnp.concatenate([row[:, c * LANES : (c + 1) * LANES] for c in range(lines)], axis=0)
        for member in range(packed_ref.shape[0]):
            packed_ref[member, i] = block
    trace = pick_trace(history[HIST - 1 : HIST, :], send)
    for r in range(trace_ref.shape[0]):
        trace_ref[r] = trace


def density_kernel(step, plan_ref, part_ref, recv_ref, gain_ref, inc_ref, self_ref, *refs):
    nodes = inc_ref.shape[1]
    place = Plan(plan_ref).place
    region, partner, group = place[0], place[1], place[2]
    last = step == STEPS - 1
    if step == 0:
        trace_ref, dens_ref, row_ref, past_ref = refs
        groups = part_ref.shape[0] // 2
        fields = []
        for h in range(2):
            total = part_ref[h]
            for g in range(1, groups):
                total = total + part_ref[2 * g + h]
            fields.append(total)
        past = jnp.concatenate(fields, axis=0)
        past_ref[...] = past
        trace = trace_ref[partner]
        rows = [past[8 * h + b : 8 * h + b + 1, :] for h in range(2) for b in range(2)]
    else:
        past_ref = refs[0]
        groups = part_ref.shape[0] // 8
        first = region * (2 * groups)
        rows = []
        for h in range(2):
            total = past_ref[8 * h + 2 * step : 8 * h + 2 * step + 2, :]
            for g in range(groups):
                total = total + part_ref[first + 2 * g + h]
            rows += [total[0:1, :], total[1:2, :]]
        trace = part_ref[(partner * groups + group) * 2][0:1, :]
    field = jnp.concatenate(rows, axis=1)
    junction = junction_of(trace, recv_ref, gain_ref, nodes)
    density = (inc_ref[step : step + 1, :] - field - junction) / self_ref[...]
    if last:
        row_refs, out_ref = refs[1:-1], refs[-1]
        for n in range(STEPS - 1):
            out_ref[n : n + 1, :] = row_refs[n][...]
        out_ref[STEPS - 1 : STEPS, :] = density
    else:
        if step > 0:
            dens_ref, row_ref = refs[1:]
        row_ref[...] = density
        for r in range(nodes // LANES):
            part = density[:, r * LANES : (r + 1) * LANES]
            dens_ref[:, r, :] = jnp.broadcast_to(part, (dens_ref.shape[0], LANES))


def body(
    history,
    incident,
    positions,
    area,
    self_weight,
    pair_target,
    pair_source,
    pair_lag,
    pair_count,
    junc_send,
    junc_recv,
    junc_gain,
    adjacency,
):
    nodes = history.shape[1]
    half = nodes // 2
    jrows = junc_send.shape[1]
    groups, regions, loops = (lax.axis_size(name) for name in ("group", "region", "loop"))
    tiles = 2 * groups
    f32 = jnp.float32
    shape = jax.ShapeDtypeStruct
    self_row = self_weight.reshape(1, nodes)
    line_rows = nodes // LANES

    given = (pair_count, pair_target, pair_source, pair_lag, adjacency)
    arrays = (positions, area.reshape(1, nodes), history, junc_send)
    plan, packed, trace = pl.pallas_call(
        prepare_kernel,
        out_shape=(
            shape((4 * pair_lag.shape[1] + STEPS + 3,), jnp.int32),
            shape((loops, STORED_ROW + HIST - FIRST_STORED, line_rows, LANES), f32),
            shape((regions, 1, jrows), f32),
        ),
        in_specs=[SMEM] * 5 + [VMEM] * 4,
        out_specs=(SMEM, VMEM, VMEM),
    )(*given, *arrays)
    sources = lax.all_to_all(packed, "loop", 0, 0, tiled=True)
    targets = lax.all_to_all(jnp.broadcast_to(positions, (groups, 3, nodes)), "group", 0, 0, tiled=True)
    traces = lax.all_to_all(trace, "region", 0, 0, tiled=True)

    def work(steps):
        return [
            pltpu.VMEM((3, half, LANES), f32),
            pltpu.VMEM((3, SUBS, nodes), f32),
            pltpu.VMEM((steps * COEFS, SUBS, nodes), f32),
            pltpu.VMEM((steps, half, LANES), f32),
        ]

    partial_fields = pl.pallas_call(
        history_kernel,
        out_shape=shape((tiles, 2 * STEPS, LANES), f32),
        in_specs=[SMEM] + [VMEM] * 2,
        out_specs=VMEM,
        scratch_shapes=work(STEPS) * 2,
        compiler_params=PAIR_GRANT,
    )(plan, targets, sources)
    plan, partial_fields, traces = lax.optimization_barrier((plan, partial_fields, traces))
    near = pl.pallas_call(
        near_kernel,
        out_shape=shape((NEAR, NEAR_COEFS, line_rows, half, LANES), f32),
        in_specs=[SMEM] + [VMEM] * 2,
        out_specs=VMEM,
        scratch_shapes=[pltpu.VMEM((3, half, LANES), f32), pltpu.VMEM((4, SUBS, nodes), f32)] * 2,
        compiler_params=NEAR_GRANT,
    )(plan, targets, sources)
    near, partial_fields = lax.optimization_barrier((near, partial_fields))
    parts = lax.all_to_all(partial_fields, "group", 0, 0, tiled=True)

    dens_shape, row_shape = shape((loops, line_rows, LANES), f32), shape((1, nodes), f32)
    rows, gathered = [], []
    past = None
    for step in range(STEPS):
        if step > 0:
            partial_fields = pl.pallas_call(
                functools.partial(step_kernel, step),
                out_shape=shape((regions * tiles, 2, LANES), f32),
                in_specs=[SMEM] + [VMEM] * (5 + step),
                out_specs=VMEM,
                scratch_shapes=[pltpu.VMEM((loops, SUBS, line_rows, LANES), f32)] + work(1) * 2,
                compiler_params=NEAR_GRANT,
            )(plan, near, targets, sources, junc_send, rows[-1], *gathered)
            parts = lax.all_to_all(partial_fields, ("region", "group"), 0, 0, tiled=True)
        operands = [plan, parts, junc_recv, junc_gain, incident, self_row]
        if step == 0:
            operands += [traces]
            out_shape = [dens_shape, row_shape, shape((2 * 2 * STEPS, LANES), f32)]
        elif step < STEPS - 1:
            operands += [past]
            out_shape = [dens_shape, row_shape]
        else:
            operands += [past] + rows
            out_shape = [shape((STEPS, nodes), f32)]
        results = pl.pallas_call(
            functools.partial(density_kernel, step),
            out_shape=out_shape,
            in_specs=[SMEM] + [VMEM] * (len(operands) - 1),
            out_specs=[VMEM] * len(out_shape),
            compiler_params=SMALL_GRANT,
        )(*operands)
        if step == 0:
            past = results[2]
        if step < STEPS - 1:
            rows.append(results[1])
            gathered.append(lax.all_to_all(results[0], "loop", 0, 0, tiled=True))
    return results[0]


def solution(mesh):
    blocks = ("region", "group", "loop")
    in_specs = (
        P(None, blocks),
        P(None, blocks),
        P(None, blocks),
        P(blocks),
        P(blocks),
        P(blocks, None),
        P(blocks, None),
        P(blocks, None),
        P(blocks),
        P(blocks, None),
        P(blocks, None),
        P(blocks, None),
        P(blocks),
    )
    return jax.shard_map(body, mesh=mesh, in_specs=in_specs, out_specs=P(None, blocks), check_vma=False)
```
